256 devices in a mesh: grp: 4 (over x), tm: 64 (over z, y, core).
Axes of the slice: x: 4, y: 4, z: 8, core: 2. Of those that a mesh axis runs over, the one named last changes fastest.
Arguments:
- signal: bfloat16 [4, 8192, 512], P('grp', 'tm'), may hold values from -16 to 16
- damping: float32 [4, 8192], P('grp', 'tm'), may hold values from 0.25 to 1, as said below
- nu_log: float32 [1024], replicated, as said below
- theta: float32 [1024], replicated, may hold values from 0 to 0.63
- in_weight: bfloat16 [512, 2048], replicated, may hold values from -0.25 to 0.25
- out_weight: bfloat16 [512, 2048], replicated, may hold values from -0.125 to 0.125
- skip_gain: float32 [512], replicated, may hold values from 0.1 to 1.9
- cotangent: bfloat16 [4, 8192, 512], P('grp', 'tm'), may hold values from -16 to 16
Outputs:
- mixed: bfloat16 [4, 8192, 512], P('grp', 'tm')
- grad_signal: bfloat16 [4, 8192, 512], P('grp', 'tm')
- grad_in: float32 [512, 2048], P(('grp', 'tm'))
- grad_out: float32 [512, 2048], P(('grp', 'tm'))
The draws below stay inside these ranges and needn't reach their ends.
Inputs may be any that keep to these rules, and one draw needn't show every extreme that they name: damping is 1 except at a few time steps of each record. exp(nu_log) lies between 0.01 / 8192 and 1/30.
All inputs are finite; a program needn't handle non-finite values.
Results may differ from the reference program's by a relative error of at most 0.0034.
Values sent between devices are 32-bit elements; how exact they have to be, the bound alone decides.
No kernel may reach another device: no remote copies, remote signals or barrier semaphores. Data moves between devices by JAX's collectives and lax.ppermute only.
A program may use at most 128 MiB of HBM per device.

```python
import math
import jax
import jax.numpy as jnp
from jax import lax

D = 512
N = 1024
TOK_DEV = 128
RECORD_COUNT = 4
TOKEN_STEPS = 8192


def draw_nu_log(key, part):
    leading_operand, trailing_operand, third = jax.random.split(key, 3)
    share = 0.5
    quick_pick = jax.random.uniform(leading_operand, (N,), jnp.float32) < share
    quick = jax.random.uniform(trailing_operand, (N,), jnp.float32, minval=1.0 / 50.0, maxval=1.0 / 30.0)
    slow_log = jax.random.uniform(third, (N,), jnp.float32, minval=math.log(0.01 / TOKEN_STEPS), maxval=math.log(1.0 / TOKEN_STEPS))
    return jnp.where(quick_pick, jnp.log(quick), slow_log).astype(jnp.float32)


def draw_damping(key, part):
    leading_operand, trailing_operand = jax.random.split(key, 2)
    pulse_count = 8
    position_list = jax.random.randint(leading_operand, (RECORD_COUNT, pulse_count), 0, TOKEN_STEPS)
    intensity_factor = jax.random.uniform(trailing_operand, (RECORD_COUNT, pulse_count), jnp.float32, minval=0.6, maxval=0.8)
    marks = position_list[:, :, None] == jnp.arange(TOKEN_STEPS, dtype=jnp.int32)[None, None, :]
    factors = jnp.where(marks, intensity_factor[:, :, None], 1.0)
    return jnp.prod(factors, axis=1).astype(jnp.float32)


def strengthened(drawn, rng, source, target, blocks, factor):
    def block_of(dim):
        return (jnp.arange(drawn.shape[dim]) // (drawn.shape[dim] // blocks)).reshape((-1,) + (1,) * (drawn.ndim - 1 - dim))

    one_side = jax.random.permutation(rng, blocks)[block_of(target)]
    far = (block_of(target) + blocks // 2) % blocks
    return jnp.where((block_of(source) == one_side) | (block_of(source) == far), factor * drawn, drawn)


def levels(stream_key, shape, cuts, low, top_value):
    level = 1.0
    for axis_at, parts in cuts:
        heights = jax.random.uniform(jax.random.fold_in(jax.random.fold_in(stream_key, 6), axis_at), (parts,), jnp.float32, low / len(cuts), top_value / len(cuts))
        level = level * jnp.repeat(jnp.exp(heights), shape[axis_at] // parts).reshape((-1,) + (1,) * (len(shape) - 1 - axis_at))
    return level


def normal_values(rng, extent, spread, most, pieces=(), held_as=jnp.bfloat16):
    values = spread * jax.random.normal(rng, extent, jnp.float32)
    if pieces:
        values = values * levels(rng, extent, pieces, -0.22, 0.18)
    return jnp.clip(values, -most, most).astype(held_as)


def bell_draw_with(key, dims, spread, limit, pieces, heavy, kind=jnp.bfloat16):
    drawn = spread * jax.random.normal(key, dims, jnp.float32)
    if pieces:
        drawn = drawn * levels(key, dims, pieces, -0.22, 0.18)
    return jnp.clip(strengthened(drawn, jax.random.fold_in(key, 3), *heavy), -limit, limit).astype(kind)


def setup_inputs(seed: int = 0) -> dict:
    key_of = jax.random.split(jax.random.key(seed), 9)
    signal = bell_draw_with(key_of[0], (RECORD_COUNT, TOKEN_STEPS, D), 1.0, 16.0, ((0, 4), (1, 64)), (1, 2, 64, 4.0))
    damping = draw_damping(jax.random.fold_in(key_of[8], 71), 0)
    nu_log = draw_nu_log(jax.random.fold_in(key_of[8], 71), 0)
    theta = jnp.clip(jax.random.uniform(key_of[3], (N,), jnp.float32, 0.0, 0.63), 0.0, 0.63)
    in_weight = normal_values(key_of[4], (D, 2 * N), D ** -0.5, 0.25)
    out_weight = normal_values(key_of[5], (D, 2 * N), (2 * N) ** -0.5, 0.125)
    skip_gain = jnp.clip(1.0 + 0.18 * jax.random.normal(key_of[6], (D,), jnp.float32), 0.1, 1.9)
    cotangent = bell_draw_with(key_of[7], (RECORD_COUNT, TOKEN_STEPS, D), 1.0, 16.0, ((0, 4), (1, 64)), (1, 2, 64, 4.0))
    return {"signal": signal, "damping": damping, "nu_log": nu_log, "theta": theta, "in_weight": in_weight, "out_weight": out_weight, "skip_gain": skip_gain, "cotangent": cotangent}


def combine(earlier, later):
    first_re, first_im, carry_re, carry_im = earlier
    second_re, second_im, next_re, next_im = later
    prod_re = second_re * first_re - second_im * first_im
    prod_im = second_re * first_im + second_im * first_re
    moved_re = second_re * carry_re - second_im * carry_im
    moved_im = second_re * carry_im + second_im * carry_re
    return (prod_re, prod_im, moved_re + next_re, moved_im + next_im)

def reference(signal, damping, nu_log, theta, in_weight, out_weight, skip_gain, cotangent):
    width = nu_log.shape[0]
    rate = jnp.exp(nu_log)
    magnitude = jnp.exp(-rate)
    lam_re = magnitude * jnp.cos(theta)
    lam_im = magnitude * jnp.sin(theta)
    scaling = jnp.sqrt(-jnp.expm1(-2.0 * rate))
    blocks = TOKEN_STEPS // TOK_DEV

    def record_pass(totals, record):
        sig_all, damp_all, up_all = record
        sig_blocks = sig_all.reshape(blocks, TOK_DEV, D)
        damp_blocks = damp_all.reshape(blocks, TOK_DEV)
        up_blocks = up_all.reshape(blocks, TOK_DEV, D)

        def forward(carry, block):
            sig, damp, upstream = block
            decay_re = damp[:, None] * lam_re
            decay_im = damp[:, None] * lam_im
            projected = jnp.dot(sig, in_weight, preferred_element_type=jnp.float32)
            drive_re = scaling * projected[:, :width]
            drive_im = scaling * projected[:, width:]
            power_re, power_im, local_re, local_im = lax.associative_scan(combine, (decay_re, decay_im, drive_re, drive_im))
            state_re = local_re + power_re * carry[0] - power_im * carry[1]
            state_im = local_im + power_re * carry[1] + power_im * carry[0]
            packed = jnp.concatenate([state_re, state_im], 1).astype(jnp.bfloat16)
            output = lax.dot_general(packed, out_weight, (((1,), (1,)), ((), ())), preferred_element_type=jnp.float32)
            output = (output + skip_gain * sig.astype(jnp.float32)).astype(jnp.bfloat16)
            grad_part = lax.dot_general(upstream, packed, (((0,), (0,)), ((), ())), preferred_element_type=jnp.float32)
            return ((state_re[-1], state_im[-1], carry[2] + grad_part), output)
        start = (jnp.zeros((width,), jnp.float32), jnp.zeros((width,), jnp.float32), totals[1])
        (_, _, acc_out), outputs = lax.scan(forward, start, (sig_blocks, damp_blocks, up_blocks))

        def backward(carry, block):
            sig, damp, upstream = block
            decay_re = damp[:, None] * lam_re
            decay_im = damp[:, None] * lam_im
            grad_packed = jnp.dot(upstream, out_weight, preferred_element_type=jnp.float32)
            shift_re = jnp.concatenate([decay_re[1:], jnp.ones((1, width), jnp.float32)], 0)
            shift_im = jnp.concatenate([-decay_im[1:], jnp.zeros((1, width), jnp.float32)], 0)
            flipped = (jnp.flip(shift_re, 0), jnp.flip(shift_im, 0), jnp.flip(grad_packed[:, :width], 0), jnp.flip(grad_packed[:, width:], 0))
            scanned = lax.associative_scan(combine, flipped)
            back_re, back_im, local_re, local_im = [jnp.flip(item, 0) for item in scanned]
            adj_re = local_re + back_re * carry[0] - back_im * carry[1]
            adj_im = local_im + back_re * carry[1] + back_im * carry[0]
            grad_drive = jnp.concatenate([scaling * adj_re, scaling * adj_im], 1).astype(jnp.bfloat16)
            grad_sig = lax.dot_general(grad_drive, in_weight, (((1,), (1,)), ((), ())), preferred_element_type=jnp.float32)
            grad_sig = (grad_sig + skip_gain * upstream.astype(jnp.float32)).astype(jnp.bfloat16)
            grad_part = lax.dot_general(sig, grad_drive, (((0,), (0,)), ((), ())), preferred_element_type=jnp.float32)
            new_re = decay_re[0] * adj_re[0] + decay_im[0] * adj_im[0]
            new_im = decay_re[0] * adj_im[0] - decay_im[0] * adj_re[0]
            return ((new_re, new_im, carry[2] + grad_part), grad_sig)
        start_back = (jnp.zeros((width,), jnp.float32), jnp.zeros((width,), jnp.float32), totals[0])
        (_, _, acc_in), grads = lax.scan(backward, start_back, (sig_blocks, damp_blocks, up_blocks), reverse=True)
        return ((acc_in, acc_out), (outputs.reshape(TOKEN_STEPS, D), grads.reshape(TOKEN_STEPS, D)))
    zero_grad = jnp.zeros((D, 2 * width), jnp.float32)
    (grad_in, grad_out), (mixed, grad_signal) = lax.scan(record_pass, (zero_grad, zero_grad), (signal, damping, cotangent))
    return (mixed, grad_signal, grad_in, grad_out)
```

```python
import jax
import jax.numpy as jnp
import numpy as np
from jax import lax
from jax.experimental import pallas as pl
from jax.experimental.pallas import tpu as pltpu
from jax.sharding import Mesh, PartitionSpec as P

X, Z, Y, C = 4, 8, 4, 2
D, N = 512, 1024
TOK = 128
T = C * TOK
W = N // C
LANES = 128
CH = W // LANES
GROUPS = T // 8
BLOCKS = Z * Y
F32, BF16 = jnp.float32, jnp.bfloat16
NT = (((1,), (1,)), ((), ()))


def ring(size, step):
    return [(i, (i + step) % size) for i in range(size)]


def cmul(ar, ai, br, bi):
    return ar * br - ai * bi, ar * bi + ai * br


def rows8():
    return lax.broadcasted_iota(jnp.int32, (8, LANES), 0)


def fwd_factors(d, i):
    dd = d * pltpu.roll(d, 1, 0)
    dddd = dd * pltpu.roll(dd, 2, 0)
    m1 = jnp.where(i >= 1, d, 0.0)
    m2 = jnp.where(i >= 2, dd, 0.0)
    m4 = jnp.where(i >= 4, dddd, 0.0)
    return m1, m2, m4


def cum_fwd(d, i):
    p = d
    for k in (1, 2, 4):
        p = jnp.where(i >= k, p * pltpu.roll(p, k, 0), p)
    return p


def cum_bwd(d, i):
    p = d
    for k in (1, 2, 4):
        p = jnp.where(i < 8 - k, p * pltpu.roll(p, 8 - k, 0), p)
    return p


def bwd_factors(d, i):
    e = pltpu.roll(d, 7, 0)
    ee = e * pltpu.roll(e, 7, 0)
    eeee = ee * pltpu.roll(ee, 6, 0)
    m1 = jnp.where(i < 7, e, 0.0)
    m2 = jnp.where(i < 6, ee, 0.0)
    m4 = jnp.where(i < 4, eeee, 0.0)
    return m1, m2, m4


def scan8(sr, si, masks, powers, backward):
    for (k, m), (pr, pi) in zip(zip((1, 2, 4), masks), powers):
        shift = 8 - k if backward else k
        rr = m * pltpu.roll(sr, shift, 0)
        ri = m * pltpu.roll(si, shift, 0)
        if backward:
            sr, si = sr + (pr * rr + pi * ri), si + (pr * ri - pi * rr)
        else:
            sr, si = sr + (pr * rr - pi * ri), si + (pr * ri + pi * rr)
    return sr, si


def powers_of(par_ref, j):
    lr = jnp.broadcast_to(par_ref[j : j + 1, :], (8, LANES))
    li = jnp.broadcast_to(par_ref[4 + j : 5 + j, :], (8, LANES))
    p1 = (lr, li)
    p2 = cmul(*p1, *p1)
    p4 = cmul(*p2, *p2)
    p8 = cmul(*p4, *p4)
    return p1, p2, p4, p8


def local_kernel(
    idx, par, damp, sig, cot, other, win_re, win_im, wout_re, wout_im,
    sig_all, cot_all, fre, fim, bre, bim, msg,
):
    c = idx[0]
    own = pl.ds(pl.multiple_of(c * TOK, TOK), TOK)
    oth = pl.ds(pl.multiple_of((1 - c) * TOK, TOK), TOK)
    sig_all[own, :] = sig[...]
    cot_all[own, :] = cot[...]
    sig_all[oth, :] = other[:, :D].astype(BF16)
    cot_all[oth, :] = other[:, D:].astype(BF16)
    s = sig_all[...]
    u = cot_all[...]
    fre[...] = jnp.dot(s, win_re[...], preferred_element_type=F32)
    fim[...] = jnp.dot(s, win_im[...], preferred_element_type=F32)
    bre[...] = jnp.dot(u, wout_re[...], preferred_element_type=F32)
    bim[...] = jnp.dot(u, wout_im[...], preferred_element_type=F32)
    i = rows8()
    pw = [powers_of(par, j) for j in range(CH)]
    gam = [jnp.broadcast_to(par[8 + j : 9 + j, :], (8, LANES)) for j in range(CH)]

    def step(g, carry):
        ff, mm, prod = carry
        rf = pl.ds(pl.multiple_of(g * 8, 8), 8)
        rb = pl.ds(pl.multiple_of((GROUPS - 1 - g) * 8, 8), 8)
        df = damp[rf, :]
        db = damp[rb, :]
        mf = fwd_factors(df, i)
        mb = bwd_factors(db, i)
        cf = cum_fwd(df, i)
        cb = cum_bwd(db, i)
        nf, nm = [], []
        for j in range(CH):
            col = pl.ds(j * LANES, LANES)
            p1, p2, p4, p8 = pw[j]
            sr, si = scan8(
                gam[j] * fre[rf, col], gam[j] * fim[rf, col], mf, (p1, p2, p4), False
            )
            fre[rf, col] = sr
            fim[rf, col] = si
            ar, ai = cmul(*p8, *ff[j])
            nf.append((sr + cf * ar, si + cf * ai))
            sr, si = scan8(bre[rb, col], bim[rb, col], mb, (p1, p2, p4), True)
            bre[rb, col] = sr
            bim[rb, col] = si
            vr, vi = cmul(p1[0], -p1[1], sr, si)
            ar, ai = cmul(p8[0], -p8[1], *mm[j])
            nm.append((db * vr + cb * ar, db * vi + cb * ai))
        return nf, nm, prod * cf

    zero = jnp.zeros((8, LANES), F32)
    start = [(zero, zero) for _ in range(CH)]
    ff, mm, prod = lax.fori_loop(0, GROUPS, step, (start, start, zero + 1.0))
    rows = (
        [ff[j][0][7:8] for j in range(CH)]
        + [ff[j][1][7:8] for j in range(CH)]
        + [mm[j][0][0:1] for j in range(CH)]
        + [mm[j][1][0:1] for j in range(CH)]
    )
    message = jnp.concatenate(rows + [jnp.broadcast_to(prod[7:8], (8, LANES))], 0)
    msg[...] = jnp.broadcast_to(message[None], msg.shape)


def local_call(idx, par, damp, sig, cot, other, in_weight, out_weight):
    whole = lambda shape: pl.BlockSpec(shape, lambda s, ix: (0,) * len(shape))
    half = lambda k: pl.BlockSpec((D, W), lambda s, ix: (0, k * C + ix[0]))
    shapes = (
        [((T, D), BF16)] * 2 + [((T, W), F32)] * 4 + [((BLOCKS, 24, LANES), F32)]
    )
    return pl.pallas_call(
        local_kernel,
        grid_spec=pltpu.PrefetchScalarGridSpec(
            num_scalar_prefetch=1,
            grid=(1,),
            in_specs=[
                whole((16, LANES)), whole((T, LANES)), whole((TOK, D)), whole((TOK, D)),
                whole((TOK, 2 * D)), half(0), half(1), half(0), half(1),
            ],
            out_specs=[whole(s) for s, _ in shapes],
        ),
        out_shape=[jax.ShapeDtypeStruct(s, t) for s, t in shapes],
        name="local",
    )(idx, par, damp, sig, cot, other, in_weight, in_weight, out_weight, out_weight)


def one_hot(order):
    r = lax.broadcasted_iota(jnp.int32, (D, D), 0)
    k = lax.broadcasted_iota(jnp.int32, (D, D), 1)
    hi, mid, z, low = r >> 7, (r >> 5) & 3, (r >> 2) & 7, r & 3
    x, y = (hi, mid) if order == "xy" else (mid, hi)
    old = x * 128 + z * 16 + y * 4 + low
    return jnp.where(old == k, 1.0, 0.0).astype(BF16)


def grads_kernel(idx, par, damp, sig, cot, fre, fim, bre, bim, got, *rest):
    outs, packed, drive = rest[:8], rest[8], rest[9]
    sr_, si_, ar_, ai_, lhs_in, lhs_out = rest[10:]
    x, y, q = idx[1], idx[2], idx[3]
    i = rows8()
    lam_r, lam_i = par[0:CH, :], par[4 : 4 + CH, :]
    pr, pi = lam_r, lam_i
    for _ in range(8):
        pr, pi = cmul(pr, pi, pr, pi)

    def joined(b, carry):
        fr, fi, mr, mi = carry
        dec = got[b, 16 : 16 + CH, :]
        tr, ti = cmul(dec * pr, dec * pi, fr, fi)
        on = b < q
        fr = jnp.where(on, tr + got[b, 0:CH, :], fr)
        fi = jnp.where(on, ti + got[b, 4 : 4 + CH, :], fi)
        e = BLOCKS - 1 - b
        dec = got[e, 16 : 16 + CH, :]
        tr, ti = cmul(dec * pr, -(dec * pi), mr, mi)
        on = e > q
        mr = jnp.where(on, tr + got[e, 8 : 8 + CH, :], mr)
        mi = jnp.where(on, ti + got[e, 12 : 12 + CH, :], mi)
        return fr, fi, mr, mi

    zero = jnp.zeros((CH, LANES), F32)
    fr, fi, mr, mi = lax.fori_loop(0, BLOCKS, joined, (zero,) * 4)
    spread = lambda a, j: jnp.broadcast_to(a[j : j + 1, :], (8, LANES))
    tabs, backs, gams, eights, ones = [], [], [], [], []
    for j in range(CH):
        p1, p2, p4, p8 = powers_of(par, j)
        tr, ti = zero8 = (jnp.ones((8, LANES), F32), jnp.zeros((8, LANES), F32))
        for bit, p in ((1, p1), (2, p2), (4, p4)):
            nr, ni = cmul(tr, ti, *p)
            on = (i & bit) != 0
            tr, ti = jnp.where(on, nr, tr), jnp.where(on, ni, ti)
        tabs.append(cmul(tr, ti, *p1))
        tr, ti = zero8
        for bit, p in ((1, p1), (2, p2), (4, p4)):
            nr, ni = cmul(tr, ti, *p)
            on = ((7 - i) & bit) != 0
            tr, ti = jnp.where(on, nr, tr), jnp.where(on, ni, ti)
        backs.append((tr, -ti))
        gams.append(jnp.broadcast_to(par[8 + j : 9 + j, :], (8, LANES)))
        ones.append(p1)

    def step(g, carry):
        ff, mm = carry
        rf = pl.ds(pl.multiple_of(g * 8, 8), 8)
        rb = pl.ds(pl.multiple_of((GROUPS - 1 - g) * 8, 8), 8)
        cf = cum_fwd(damp[rf, :], i)
        db = damp[rb, :]
        e = jnp.where(i < 7, pltpu.roll(db, 7, 0), 1.0)
        cb = cum_bwd(e, i)
        nf, nm = [], []
        for j in range(CH):
            col = pl.ds(j * LANES, LANES)
            colb = pl.ds(W + j * LANES, LANES)
            tr, ti = cmul(*tabs[j], *ff[j])
            sr = fre[rf, col] + cf * tr
            si = fim[rf, col] + cf * ti
            sr_[rf, col] = sr
            sr_[rf, colb] = si
            nf.append((spread(sr, 7), spread(si, 7)))
            tr, ti = cmul(*backs[j], *mm[j])
            vr = bre[rb, col] + cb * tr
            vi = bim[rb, col] + cb * ti
            ar_[rb, col] = gams[j] * vr
            ar_[rb, colb] = gams[j] * vi
            tr, ti = cmul(ones[j][0], -ones[j][1], vr, vi)
            nm.append((spread(db * tr, 0), spread(db * ti, 0)))
        return nf, nm

    lax.fori_loop(
        0, GROUPS, step,
        (
            [(spread(fr, j), spread(fi, j)) for j in range(CH)],
            [(spread(mr, j), spread(mi, j)) for j in range(CH)],
        ),
    )
    packed[...] = sr_[...].astype(BF16)
    drive[...] = ar_[...].astype(BF16)
    lhs_in[...] = lax.dot_general(
        one_hot("xy"), sig[...], NT, preferred_element_type=F32
    ).astype(BF16)
    lhs_out[...] = lax.dot_general(
        one_hot("yx"), cot[...], NT, preferred_element_type=F32
    ).astype(BF16)
    for d in range(4):
        rows = pl.ds(pl.multiple_of(((x + d) & 3) * 128, 128), 128)
        outs[d][...] = jnp.dot(lhs_in[rows, :], drive[...], preferred_element_type=F32)
        rows = pl.ds(pl.multiple_of(((y + d) & 3) * 128, 128), 128)
        outs[4 + d][...] = jnp.dot(lhs_out[rows, :], packed[...], preferred_element_type=F32)


def grads_call(idx, par, damp, sig, cot, fre, fim, bre, bim, got):
    whole = lambda shape: pl.BlockSpec(shape, lambda s, ix: (0,) * len(shape))
    shapes = [((128, 2 * W), F32)] * 8 + [((T, 2 * W), BF16)] * 2
    return pl.pallas_call(
        grads_kernel,
        grid_spec=pltpu.PrefetchScalarGridSpec(
            num_scalar_prefetch=1,
            grid=(1,),
            in_specs=[
                whole((16, LANES)), whole((T, LANES)), whole((T, D)), whole((T, D)),
                whole((T, W)), whole((T, W)), whole((T, W)), whole((T, W)),
                whole((BLOCKS, 24, LANES)),
            ],
            out_specs=[whole(s) for s, _ in shapes],
            scratch_shapes=[
                pltpu.VMEM((T, 2 * W), F32), pltpu.VMEM((8, LANES), F32),
                pltpu.VMEM((T, 2 * W), F32), pltpu.VMEM((8, LANES), F32),
                pltpu.VMEM((D, T), BF16), pltpu.VMEM((D, T), BF16),
            ],
        ),
        out_shape=[jax.ShapeDtypeStruct(s, t) for s, t in shapes],
        name="grads",
    )(idx, par, damp, sig, cot, fre, fim, bre, bim, got)


def rows_kernel(idx, packed, drive, win_re, win_im, wout_re, wout_im, own, oth):
    c = idx[0]
    for out, at in ((own, c), (oth, 1 - c)):
        rows = pl.ds(pl.multiple_of(at * TOK, TOK), TOK)
        out[:, :D] = lax.dot_general(
            packed[rows, :W], wout_re[...], NT, preferred_element_type=F32
        ) + lax.dot_general(packed[rows, W:], wout_im[...], NT, preferred_element_type=F32)
        out[:, D:] = lax.dot_general(
            drive[rows, :W], win_re[...], NT, preferred_element_type=F32
        ) + lax.dot_general(drive[rows, W:], win_im[...], NT, preferred_element_type=F32)


def rows_call(idx, packed, drive, in_weight, out_weight):
    whole = lambda shape: pl.BlockSpec(shape, lambda s, ix: (0,) * len(shape))
    half = lambda k: pl.BlockSpec((D, W), lambda s, ix: (0, k * C + ix[0]))
    return pl.pallas_call(
        rows_kernel,
        grid_spec=pltpu.PrefetchScalarGridSpec(
            num_scalar_prefetch=1,
            grid=(1,),
            in_specs=[whole((T, 2 * W)), whole((T, 2 * W)), half(0), half(1), half(0), half(1)],
            out_specs=[whole((TOK, 2 * D))] * 2,
        ),
        out_shape=[jax.ShapeDtypeStruct((TOK, 2 * D), F32)] * 2,
        name="rows",
    )(idx, packed, drive, in_weight, in_weight, out_weight, out_weight)


def sum_kernel(slot, idx, a, b, c, d, *outs):
    at = idx[slot]
    total = a[...] + b[...] + c[...] + d[...]
    scratch = outs[4]
    scratch[...] = total
    for k in range(4):
        outs[k][...] = scratch[pl.ds(pl.multiple_of(((at + k) & 3) * 32, 32), 32), :]


def sum_call(slot, idx, parts):
    whole = lambda shape: pl.BlockSpec(shape, lambda s, ix: (0,) * len(shape))
    return pl.pallas_call(
        lambda *refs: sum_kernel(slot, *refs),
        grid_spec=pltpu.PrefetchScalarGridSpec(
            num_scalar_prefetch=1,
            grid=(1,),
            in_specs=[whole((128, 2 * W))] * 4,
            out_specs=[whole((32, 2 * W))] * 4,
            scratch_shapes=[pltpu.VMEM((128, 2 * W), F32)],
        ),
        out_shape=[jax.ShapeDtypeStruct((32, 2 * W), F32)] * 4,
        name="sums",
    )(idx, *parts)


def body(signal, damping, nu_log, theta, in_weight, out_weight, skip_gain, cotangent):
    x, z = lax.axis_index("x"), lax.axis_index("z")
    y, c = lax.axis_index("y"), lax.axis_index("c")
    idx = jnp.stack([c, x, y, z * Y + y]).astype(jnp.int32)
    rate = jnp.exp(nu_log)
    magnitude = jnp.exp(-rate)
    par = jnp.concatenate(
        [magnitude * jnp.cos(theta), magnitude * jnp.sin(theta), jnp.sqrt(-jnp.expm1(-2.0 * rate)), rate]
    ).reshape(4, C, CH, LANES)
    par = lax.dynamic_index_in_dim(par, c, 1, False).reshape(16, LANES)
    sig, cot = signal[0], cotangent[0]
    wide = jnp.concatenate([sig, cot], 1).astype(F32)
    swap = ring(C, 1)
    other = lax.ppermute(wide, "c", swap)
    damp_other = lax.ppermute(damping, "c", swap)
    damp = jnp.where(
        c == 0,
        jnp.concatenate([damping[0], damp_other[0]]),
        jnp.concatenate([damp_other[0], damping[0]]),
    )
    damp = jnp.broadcast_to(damp[:, None], (T, LANES))
    sig_all, cot_all, fre, fim, bre, bim, msg = local_call(
        idx, par, damp, sig, cot, other, in_weight, out_weight
    )
    got = lax.all_to_all(msg, ("z", "y"), 0, 0)
    made = grads_call(idx, par, damp, sig_all, cot_all, fre, fim, bre, bim, got)
    one, two, packed, drive = made[:4], made[4:8], made[8], made[9]

    def hop(parts, axis, size):
        return [parts[0]] + [
            lax.ppermute(parts[d], axis, ring(size, d)) for d in (1, 3, 2)
        ]

    one = hop(one, "x", X)
    two = hop(two, "y", Y)
    own, oth = rows_call(idx, packed, drive, in_weight, out_weight)
    own = own + lax.ppermute(oth, "c", swap)
    gain = jnp.concatenate([skip_gain, skip_gain])
    rows = (own + gain * wide).astype(BF16)
    one = hop(sum_call(2, idx, one), "y", Y)
    two = hop(sum_call(1, idx, two), "x", X)
    small = jnp.concatenate(
        [
            (one[0] + one[1] + one[2] + one[3]).reshape(Z, 4, 2 * W),
            (two[0] + two[1] + two[2] + two[3]).reshape(Z, 4, 2 * W),
        ],
        1,
    )
    small = lax.all_to_all(small, "z", 0, 0).sum(0).reshape(2, C, 2, 2 * W)
    keep = lax.dynamic_index_in_dim(small, c, 1, False)
    send = lax.dynamic_index_in_dim(small, 1 - c, 1, False)
    come = lax.ppermute(send, "c", swap)
    first = jnp.where(c == 0, keep, come).reshape(2, 2, 2, 1, W)
    second = jnp.where(c == 0, come, keep).reshape(2, 2, 2, 1, W)
    full = jnp.concatenate([first, second], 3).reshape(2, 2, 2 * N)
    return rows[None, :, :D], rows[None, :, D:], full[0], full[1]


def solution(mesh):
    grid = Mesh(np.asarray(mesh.devices).reshape(X, Z, Y, C), ("x", "z", "y", "c"))
    tm = ("z", "y", "c")
    placed = (P("x", tm, None), P("x", tm), P(), P(), P(), P(), P(), P("x", tm, None))
    rows = P(("x",) + tm, None)
    return jax.shard_map(
        body,
        mesh=grid,
        in_specs=placed,
        out_specs=(P("x", tm, None), P("x", tm, None), rows, rows),
        check_vma=False,
    )
```

```python
import jax
import jax.numpy as jnp
import numpy as np
from jax import lax
from jax.experimental import pallas as pl
from jax.experimental.pallas import tpu as pltpu
from jax.sharding import Mesh, PartitionSpec as P


X, Z, Y, C = 4, 8, 4, 2
D, N = 512, 1024
TOK = 128
T = C * TOK
W = N // C
LANES = 128
CH = W // LANES
GROUPS = T // 8
BLOCKS = Z * Y
F32, BF16 = jnp.float32, jnp.bfloat16
NT = (((1,), (1,)), ((), ()))
VMEM = 20 << 20
LOCAL_VMEM = 49 << 20
MSG = 4 * W + LANES


def ring(size, step):
    return [(i, (i + step) % size) for i in range(size)]


def cmul(ar, ai, br, bi):
    return ar * br - ai * bi, ar * bi + ai * br


def rows8():
    return lax.broadcasted_iota(jnp.int32, (8, LANES), 0)


def fwd_factors(d, i):
    dd = d * pltpu.roll(d, 1, 0)
    dddd = dd * pltpu.roll(dd, 2, 0)
    m1 = jnp.where(i >= 1, d, 0.0)
    m2 = jnp.where(i >= 2, dd, 0.0)
    m4 = jnp.where(i >= 4, dddd, 0.0)
    return m1, m2, m4


def cum_fwd(d, i):
    p = d
    for k in (1, 2, 4):
        p = jnp.where(i >= k, p * pltpu.roll(p, k, 0), p)
    return p


def cum_bwd(d, i):
    p = d
    for k in (1, 2, 4):
        p = jnp.where(i < 8 - k, p * pltpu.roll(p, 8 - k, 0), p)
    return p


def bwd_factors(d, i):
    e = pltpu.roll(d, 7, 0)
    ee = e * pltpu.roll(e, 7, 0)
    eeee = ee * pltpu.roll(ee, 6, 0)
    m1 = jnp.where(i < 7, e, 0.0)
    m2 = jnp.where(i < 6, ee, 0.0)
    m4 = jnp.where(i < 4, eeee, 0.0)
    return m1, m2, m4


def scan8(sr, si, masks, powers, backward):
    for (k, m), (pr, pi) in zip(zip((1, 2, 4), masks), powers):
        shift = 8 - k if backward else k
        rr = m * pltpu.roll(sr, shift, 0)
        ri = m * pltpu.roll(si, shift, 0)
        if backward:
            sr, si = sr + (pr * rr + pi * ri), si + (pr * ri - pi * rr)
        else:
            sr, si = sr + (pr * rr - pi * ri), si + (pr * ri + pi * rr)
    return sr, si


def powers_of(par_ref, j):
    lr = jnp.broadcast_to(par_ref[j : j + 1, :], (8, LANES))
    li = jnp.broadcast_to(par_ref[4 + j : 5 + j, :], (8, LANES))
    p1 = (lr, li)
    p2 = cmul(*p1, *p1)
    p4 = cmul(*p2, *p2)
    p8 = cmul(*p4, *p4)
    return p1, p2, p4, p8


def local_kernel(
    idx, par, mine, other, win, wout,
    sig_all, cot_all, fre, fim, bre, bim, msg, damp, weights, sems,
):
    c = idx[0]
    copies = []
    for k in range(4):
        cols = pl.ds(pl.multiple_of((k % 2) * N + c * W, W), W)
        copies.append(
            pltpu.make_async_copy(
                (win, wout)[k // 2].at[:, cols], weights.at[k], sems.at[k]
            )
        )
        copies[k].start()
    own = pl.ds(pl.multiple_of(c * TOK, TOK), TOK)
    oth = pl.ds(pl.multiple_of((1 - c) * TOK, TOK), TOK)
    for at, half in ((own, mine), (oth, other)):
        damp[at, :] = jnp.broadcast_to(half[TOK : TOK + 1, :LANES], (TOK, LANES)).T
        sig_all[at, :] = half[:TOK, :D].astype(BF16)
        cot_all[at, :] = half[:TOK, D:].astype(BF16)
    s = sig_all[...]
    u = cot_all[...]
    for k, (lhs, out) in enumerate(((s, fre), (s, fim), (u, bre), (u, bim))):
        copies[k].wait()
        out[...] = jnp.dot(lhs, weights[k], preferred_element_type=F32)
    i = rows8()
    pw = [powers_of(par, j) for j in range(CH)]
    gam = [jnp.broadcast_to(par[8 + j : 9 + j, :], (8, LANES)) for j in range(CH)]

    def step(g, carry):
        ff, mm, prod = carry
        rf = pl.ds(pl.multiple_of(g * 8, 8), 8)
        rb = pl.ds(pl.multiple_of((GROUPS - 1 - g) * 8, 8), 8)
        df = damp[rf, :]
        db = damp[rb, :]
        mf = fwd_factors(df, i)
        mb = bwd_factors(db, i)
        cf = cum_fwd(df, i)
        cb = cum_bwd(db, i)
        nf, nm = [], []
        for j in range(CH):
            col = pl.ds(j * LANES, LANES)
            p1, p2, p4, p8 = pw[j]
            sr, si = scan8(
                gam[j] * fre[rf, col], gam[j] * fim[rf, col], mf, (p1, p2, p4), False
            )
            fre[rf, col] = sr
            fim[rf, col] = si
            ar, ai = cmul(*p8, *ff[j])
            nf.append((sr + cf * ar, si + cf * ai))
            sr, si = scan8(bre[rb, col], bim[rb, col], mb, (p1, p2, p4), True)
            bre[rb, col] = sr
            bim[rb, col] = si
            vr, vi = cmul(p1[0], -p1[1], sr, si)
            ar, ai = cmul(p8[0], -p8[1], *mm[j])
            nm.append((db * vr + cb * ar, db * vi + cb * ai))
        return nf, nm, prod * cf

    zero = jnp.zeros((8, LANES), F32)
    start = [(zero, zero) for _ in range(CH)]
    ff, mm, prod = lax.fori_loop(0, GROUPS, step, (start, start, zero + 1.0))
    rows = (
        [ff[j][0][7:8] for j in range(CH)]
        + [ff[j][1][7:8] for j in range(CH)]
        + [mm[j][0][0:1] for j in range(CH)]
        + [mm[j][1][0:1] for j in range(CH)]
        + [prod[7:8]]
    )
    for k, row in enumerate(rows):
        msg[:, :, k * LANES : (k + 1) * LANES] = jnp.broadcast_to(
            row[None], (BLOCKS, 1, LANES)
        )


def local_call(idx, par, mine, other, in_weight, out_weight):
    shapes = (
        [((T, D), BF16)] * 2 + [((T, W), F32)] * 4
        + [((BLOCKS, 1, MSG), F32), ((T, LANES), F32)]
    )
    far = pl.BlockSpec(memory_space=pltpu.HBM)
    return pl.pallas_call(
        local_kernel,
        grid_spec=pltpu.PrefetchScalarGridSpec(
            num_scalar_prefetch=1,
            grid=(1,),
            in_specs=[
                whole((16, LANES)), whole((TOK + 8, 2 * D)), whole((TOK + 8, 2 * D)), far, far,
            ],
            out_specs=[whole(s) for s, _ in shapes],
            scratch_shapes=[pltpu.VMEM((4, D, W), BF16), pltpu.SemaphoreType.DMA((4,))],
        ),
        out_shape=[jax.ShapeDtypeStruct(s, t) for s, t in shapes],
        compiler_params=params(LOCAL_VMEM),
        name="local",
    )(idx, par, mine, other, in_weight, out_weight)


def one_hot(order):
    r = lax.broadcasted_iota(jnp.int32, (D, D), 0)
    k = lax.broadcasted_iota(jnp.int32, (D, D), 1)
    hi, mid, z, low = r >> 7, (r >> 5) & 3, (r >> 2) & 7, r & 3
    x, y = (hi, mid) if order == "xy" else (mid, hi)
    old = x * 128 + z * 16 + y * 4 + low
    return jnp.where(old == k, 1.0, 0.0).astype(BF16)


def grads_kernel(
    idx, par, damp, sig, cot, fre, fim, bre, bim, got,
    first, second, packed, drive, lhs_in, lhs_out, sr_, ar_,
):
    x, y, q = idx[1], idx[2], idx[3]
    i = rows8()
    blocks = []
    for j in range(CH):
        pr, pi = powers_of(par, j)[3]
        for _ in range(5):
            pr, pi = cmul(pr, pi, pr, pi)
        blocks.append((pr, pi))

    def row(b, k):
        return jnp.broadcast_to(got[b, :, k * LANES : (k + 1) * LANES], (8, LANES))

    def joined(b, carry):
        ff, mm = carry
        e = BLOCKS - 1 - b
        dec_f, dec_m = row(b, 4 * CH), row(e, 4 * CH)
        nf, nm = [], []
        for j in range(CH):
            pr, pi = blocks[j]
            tr, ti = cmul(dec_f * pr, dec_f * pi, *ff[j])
            on = b < q
            nf.append((
                jnp.where(on, tr + row(b, j), ff[j][0]),
                jnp.where(on, ti + row(b, CH + j), ff[j][1]),
            ))
            tr, ti = cmul(dec_m * pr, -(dec_m * pi), *mm[j])
            on = e > q
            nm.append((
                jnp.where(on, tr + row(e, 2 * CH + j), mm[j][0]),
                jnp.where(on, ti + row(e, 3 * CH + j), mm[j][1]),
            ))
        return nf, nm

    zero = jnp.zeros((8, LANES), F32)
    ff, mm = lax.fori_loop(0, BLOCKS, joined, ([(zero, zero)] * CH, [(zero, zero)] * CH))
    spread = lambda a, j: jnp.broadcast_to(a[j : j + 1, :], (8, LANES))
    tabs, backs, gams, ones = [], [], [], []
    for j in range(CH):
        p1, p2, p4, _ = powers_of(par, j)
        tr, ti = zero8 = (jnp.ones((8, LANES), F32), jnp.zeros((8, LANES), F32))
        for bit, p in ((1, p1), (2, p2), (4, p4)):
            nr, ni = cmul(tr, ti, *p)
            on = (i & bit) != 0
            tr, ti = jnp.where(on, nr, tr), jnp.where(on, ni, ti)
        tabs.append(cmul(tr, ti, *p1))
        tr, ti = zero8
        for bit, p in ((1, p1), (2, p2), (4, p4)):
            nr, ni = cmul(tr, ti, *p)
            on = ((7 - i) & bit) != 0
            tr, ti = jnp.where(on, nr, tr), jnp.where(on, ni, ti)
        backs.append((tr, -ti))
        gams.append(jnp.broadcast_to(par[8 + j : 9 + j, :], (8, LANES)))
        ones.append(p1)

    def step(g, carry):
        ff, mm = carry
        rf = pl.ds(pl.multiple_of(g * 8, 8), 8)
        rb = pl.ds(pl.multiple_of((GROUPS - 1 - g) * 8, 8), 8)
        cf = cum_fwd(damp[rf, :], i)
        db = damp[rb, :]
        e = jnp.where(i < 7, pltpu.roll(db, 7, 0), 1.0)
        cb = cum_bwd(e, i)
        nf, nm = [], []
        for j in range(CH):
            col = pl.ds(j * LANES, LANES)
            colb = pl.ds(W + j * LANES, LANES)
            tr, ti = cmul(*tabs[j], *ff[j])
            sr = fre[rf, col] + cf * tr
            si = fim[rf, col] + cf * ti
            sr_[rf, col] = sr
            sr_[rf, colb] = si
            nf.append((spread(sr, 7), spread(si, 7)))
            tr, ti = cmul(*backs[j], *mm[j])
            vr = bre[rb, col] + cb * tr
            vi = bim[rb, col] + cb * ti
            ar_[rb, col] = gams[j] * vr
            ar_[rb, colb] = gams[j] * vi
            tr, ti = cmul(ones[j][0], -ones[j][1], vr, vi)
            nm.append((spread(db * tr, 0), spread(db * ti, 0)))
        return nf, nm

    lax.fori_loop(0, GROUPS, step, (ff, mm))
    packed[...] = sr_[...].astype(BF16)
    drive[...] = ar_[...].astype(BF16)
    lhs_in[...] = lax.dot_general(
        one_hot("xy"), sig[...], NT, preferred_element_type=F32
    ).astype(BF16)
    lhs_out[...] = lax.dot_general(
        one_hot("yx"), cot[...], NT, preferred_element_type=F32
    ).astype(BF16)
    first[...] = jnp.dot(lhs_in[part(x, 2), :], drive[...], preferred_element_type=F32)
    second[...] = jnp.dot(lhs_out[part(y, 2), :], packed[...], preferred_element_type=F32)


def part(at, d):
    return pl.ds(pl.multiple_of(((at + d) & 3) * 128, 128), 128)


def params(limit=VMEM):
    return pltpu.CompilerParams(vmem_limit_bytes=limit)


def whole(shape):
    return pl.BlockSpec(shape, lambda s, ix: (0,) * len(shape))


def grads_call(idx, par, damp, sig, cot, fre, fim, bre, bim, got):
    shapes = [((128, 2 * W), F32)] * 2 + [((T, 2 * W), BF16)] * 2 + [((D, T), BF16)] * 2
    return pl.pallas_call(
        grads_kernel,
        grid_spec=pltpu.PrefetchScalarGridSpec(
            num_scalar_prefetch=1,
            grid=(1,),
            in_specs=[
                whole((16, LANES)), whole((T, LANES)), whole((T, D)), whole((T, D)),
                whole((T, W)), whole((T, W)), whole((T, W)), whole((T, W)),
                whole((BLOCKS, 1, MSG)),
            ],
            out_specs=[whole(s) for s, _ in shapes],
            scratch_shapes=[pltpu.VMEM((T, 2 * W), F32), pltpu.VMEM((T, 2 * W), F32)],
        ),
        out_shape=[jax.ShapeDtypeStruct(s, t) for s, t in shapes],
        compiler_params=params(),
        name="grads",
    )(idx, par, damp, sig, cot, fre, fim, bre, bim, got)


def second_kernel(idx, packed, drive, lhs_in, lhs_out, first1, second1, first3, second3):
    x, y = idx[1], idx[2]
    for d, first, second in ((1, first1, second1), (3, first3, second3)):
        first[...] = jnp.dot(lhs_in[part(x, d), :], drive[...], preferred_element_type=F32)
        second[...] = jnp.dot(lhs_out[part(y, d), :], packed[...], preferred_element_type=F32)


def second_call(idx, packed, drive, lhs_in, lhs_out):
    return pl.pallas_call(
        second_kernel,
        grid_spec=pltpu.PrefetchScalarGridSpec(
            num_scalar_prefetch=1,
            grid=(1,),
            in_specs=[whole((T, 2 * W)), whole((T, 2 * W)), whole((D, T)), whole((D, T))],
            out_specs=[whole((128, 2 * W))] * 4,
        ),
        out_shape=[jax.ShapeDtypeStruct((128, 2 * W), F32)] * 4,
        compiler_params=params(),
        name="second",
    )(idx, packed, drive, lhs_in, lhs_out)


def rows_kernel(
    idx, packed, drive, lhs_in, lhs_out, win_re, win_im, wout_re, wout_im,
    own, oth, first, second,
):
    c, x, y = idx[0], idx[1], idx[2]
    first[...] = jnp.dot(lhs_in[part(x, 0), :], drive[...], preferred_element_type=F32)
    second[...] = jnp.dot(lhs_out[part(y, 0), :], packed[...], preferred_element_type=F32)
    for out, at in ((own, c), (oth, 1 - c)):
        rows = pl.ds(pl.multiple_of(at * TOK, TOK), TOK)
        out[:, :D] = lax.dot_general(
            packed[rows, :W], wout_re[...], NT, preferred_element_type=F32
        ) + lax.dot_general(packed[rows, W:], wout_im[...], NT, preferred_element_type=F32)
        out[:, D:] = lax.dot_general(
            drive[rows, :W], win_re[...], NT, preferred_element_type=F32
        ) + lax.dot_general(drive[rows, W:], win_im[...], NT, preferred_element_type=F32)


def rows_call(idx, packed, drive, lhs_in, lhs_out, in_weight, out_weight):
    half = lambda k: pl.BlockSpec((D, W), lambda s, ix: (0, k * C + ix[0]))
    return pl.pallas_call(
        rows_kernel,
        grid_spec=pltpu.PrefetchScalarGridSpec(
            num_scalar_prefetch=1,
            grid=(1,),
            in_specs=[
                whole((T, 2 * W)), whole((T, 2 * W)), whole((D, T)), whole((D, T)),
                half(0), half(1), half(0), half(1),
            ],
            out_specs=[whole((TOK, 2 * D))] * 4,
        ),
        out_shape=[jax.ShapeDtypeStruct((TOK, 2 * D), F32)] * 4,
        compiler_params=params(),
        name="rows",
    )(idx, packed, drive, lhs_in, lhs_out, in_weight, in_weight, out_weight, out_weight)


def gathered(parts, at):
    out = []
    for k in range(4):
        first = ((at + k) & 3) * 32
        out.append(sum(lax.dynamic_slice(p, (first, 0), (32, 2 * W)) for p in parts))
    return out


def joined_kernel(a0, a1, a2, a3, b0, b1, b2, b3, out):
    for k, parts in enumerate(((a0, a1, a2, a3), (b0, b1, b2, b3))):
        total = parts[0][...] + parts[1][...] + parts[2][...] + parts[3][...]
        out[:, 4 * k : 4 * k + 4, :] = total.reshape(Z, 4, 2 * W)


def joined_call(one, two):
    return pl.pallas_call(
        joined_kernel,
        out_shape=jax.ShapeDtypeStruct((Z, 8, 2 * W), F32),
        compiler_params=params(),
        name="joined",
    )(*one, *two)


def body(signal, damping, nu_log, theta, in_weight, out_weight, skip_gain, cotangent):
    x, z = lax.axis_index("x"), lax.axis_index("z")
    y, c = lax.axis_index("y"), lax.axis_index("c")
    idx = jnp.stack([c, x, y, z * Y + y]).astype(jnp.int32)
    rate = jnp.exp(nu_log)
    magnitude = jnp.exp(-rate)
    par = jnp.concatenate(
        [magnitude * jnp.cos(theta), magnitude * jnp.sin(theta), jnp.sqrt(-jnp.expm1(-2.0 * rate)), rate]
    ).reshape(4, C, CH, LANES)
    par = lax.dynamic_index_in_dim(par, c, 1, False).reshape(16, LANES)
    sig, cot = signal[0], cotangent[0]
    wide = jnp.concatenate([sig, cot], 1).astype(F32)
    mine = jnp.concatenate([wide, jnp.pad(damping, ((0, 7), (0, 2 * D - TOK)))], 0)
    swap = ring(C, 1)
    other = lax.ppermute(mine, "c", swap)
    sig_all, cot_all, fre, fim, bre, bim, msg, damp = local_call(
        idx, par, mine, other, in_weight, out_weight
    )
    got = lax.all_to_all(msg, ("z", "y"), 0, 0)
    first2, second2, packed, drive, lhs_in, lhs_out = grads_call(
        idx, par, damp, sig_all, cot_all, fre, fim, bre, bim, got
    )

    def hop(part, axis, d):
        return lax.ppermute(part, axis, ring(4, d))

    one, two = [hop(first2, "x", 2)], [hop(second2, "y", 2)]
    first1, second1, first3, second3 = second_call(idx, packed, drive, lhs_in, lhs_out)
    one += [hop(first1, "x", 1), hop(first3, "x", 3)]
    two += [hop(second1, "y", 1), hop(second3, "y", 3)]
    own, oth, first, second = rows_call(
        idx, packed, drive, lhs_in, lhs_out, in_weight, out_weight
    )
    own = own + lax.ppermute(oth, "c", swap)
    gain = jnp.concatenate([skip_gain, skip_gain])
    rows = (own + gain * mine[:TOK]).astype(BF16)
    one = gathered([first] + one, y)
    one = [one[0]] + [hop(one[d], "y", d) for d in (2, 1, 3)]
    two = gathered([second] + two, x)
    two = [two[0]] + [hop(two[d], "x", d) for d in (2, 1, 3)]
    small = joined_call(one, two)
    small = lax.all_to_all(small, "z", 0, 0).sum(0).reshape(2, C, 2, 2 * W)
    keep = lax.dynamic_index_in_dim(small, c, 1, False)
    send = lax.dynamic_index_in_dim(small, 1 - c, 1, False)
    come = lax.ppermute(send, "c", swap)
    first = jnp.where(c == 0, keep, come).reshape(2, 2, 2, 1, W)
    second = jnp.where(c == 0, come, keep).reshape(2, 2, 2, 1, W)
    full = jnp.concatenate([first, second], 3).reshape(2, 2, 2 * N)
    return rows[None, :, :D], rows[None, :, D:], full[0], full[1]


def solution(mesh):
    grid = Mesh(np.asarray(mesh.devices).reshape(X, Z, Y, C), ("x", "z", "y", "c"))
    tm = ("z", "y", "c")
    placed = (P("x", tm, None), P("x", tm), P(), P(), P(), P(), P(), P("x", tm, None))
    rows = P(("x",) + tm, None)

    return jax.shard_map(
        body,
        mesh=grid,
        in_specs=placed,
        out_specs=(P("x", tm, None), P("x", tm, None), rows, rows),
        check_vma=False,
    )
```

```python
import jax
import jax.numpy as jnp
import numpy as np
from jax import lax
from jax.experimental import pallas as pl
from jax.experimental.pallas import tpu as pltpu
from jax.sharding import Mesh, PartitionSpec as P


X, Z, Y, C = 4, 8, 4, 2
D, N = 512, 1024
TOK = 128
T = C * TOK
W = N // C
H = W // 2
LANES = 128
CH = W // LANES
GROUPS = T // 8
BLOCKS = Z * Y
F32, BF16 = jnp.float32, jnp.bfloat16
NT = (((1,), (1,)), ((), ()))
VMEM = 24 << 20
PAIR_VMEM = 24 << 20
LOCAL_VMEM = 51 << 20
MSG = 4 * W + LANES


def ring(size, step):
    return [(i, (i + step) % size) for i in range(size)]


def cmul(ar, ai, br, bi):
    return ar * br - ai * bi, ar * bi + ai * br


def rows8():
    return lax.broadcasted_iota(jnp.int32, (8, LANES), 0)


def fwd_factors(d, i):
    dd = d * pltpu.roll(d, 1, 0)
    dddd = dd * pltpu.roll(dd, 2, 0)
    m1 = jnp.where(i >= 1, d, 0.0)
    m2 = jnp.where(i >= 2, dd, 0.0)
    m4 = jnp.where(i >= 4, dddd, 0.0)
    return m1, m2, m4


def cum_fwd(d, i):
    p = d
    for k in (1, 2, 4):
        p = jnp.where(i >= k, p * pltpu.roll(p, k, 0), p)
    return p


def cum_bwd(d, i):
    p = d
    for k in (1, 2, 4):
        p = jnp.where(i < 8 - k, p * pltpu.roll(p, 8 - k, 0), p)
    return p


def bwd_factors(d, i):
    e = pltpu.roll(d, 7, 0)
    ee = e * pltpu.roll(e, 7, 0)
    eeee = ee * pltpu.roll(ee, 6, 0)
    m1 = jnp.where(i < 7, e, 0.0)
    m2 = jnp.where(i < 6, ee, 0.0)
    m4 = jnp.where(i < 4, eeee, 0.0)
    return m1, m2, m4


def scan8(sr, si, masks, powers, backward):
    for (k, m), (pr, pi) in zip(zip((1, 2, 4), masks), powers):
        shift = 8 - k if backward else k
        rr = m * pltpu.roll(sr, shift, 0)
        ri = m * pltpu.roll(si, shift, 0)
        if backward:
            sr, si = sr + (pr * rr + pi * ri), si + (pr * ri - pi * rr)
        else:
            sr, si = sr + (pr * rr - pi * ri), si + (pr * ri + pi * rr)
    return sr, si


def powers_of(par_ref, j):
    lr = jnp.broadcast_to(par_ref[j : j + 1, :], (8, LANES))
    li = jnp.broadcast_to(par_ref[4 + j : 5 + j, :], (8, LANES))
    p1 = (lr, li)
    p2 = cmul(*p1, *p1)
    p4 = cmul(*p2, *p2)
    p8 = cmul(*p4, *p4)
    return p1, p2, p4, p8


def local_kernel(
    idx, par, mine, other, win, wout, msg,
    sig_all, cot_all, fre, fim, bre, bim, damp, weights, sems,
):
    c = idx[0]
    copies = []
    for k in range(4):
        cols = pl.ds(pl.multiple_of((k % 2) * N + c * W, W), W)
        copies.append(
            pltpu.make_async_copy(
                (win, wout)[k // 2].at[:, cols], weights.at[k], sems.at[k]
            )
        )
        copies[k].start()
    own = pl.ds(pl.multiple_of(c * TOK, TOK), TOK)
    oth = pl.ds(pl.multiple_of((1 - c) * TOK, TOK), TOK)
    for at, half in ((own, mine), (oth, other)):
        damp[at, :] = jnp.broadcast_to(half[TOK : TOK + 1, :LANES], (TOK, LANES)).T
        sig_all[at, :] = half[:TOK, :D].astype(BF16)
        cot_all[at, :] = half[:TOK, D:].astype(BF16)
    s = sig_all[...]
    u = cot_all[...]
    for k, (lhs, out) in enumerate(((s, fre), (s, fim), (u, bre), (u, bim))):
        copies[k].wait()
        out[...] = jnp.dot(lhs, weights[k], preferred_element_type=F32)
    i = rows8()
    pw = [powers_of(par, j) for j in range(CH)]
    gam = [jnp.broadcast_to(par[8 + j : 9 + j, :], (8, LANES)) for j in range(CH)]

    def step(g, carry):
        ff, mm, prod = carry
        rf = pl.ds(pl.multiple_of(g * 8, 8), 8)
        rb = pl.ds(pl.multiple_of((GROUPS - 1 - g) * 8, 8), 8)
        df = damp[rf, :]
        db = damp[rb, :]
        mf = fwd_factors(df, i)
        mb = bwd_factors(db, i)
        cf = cum_fwd(df, i)
        cb = cum_bwd(db, i)
        nf, nm = [], []
        for j in range(CH):
            col = pl.ds(j * LANES, LANES)
            p1, p2, p4, p8 = pw[j]
            sr, si = scan8(
                gam[j] * fre[rf, col], gam[j] * fim[rf, col], mf, (p1, p2, p4), False
            )
            ar, ai = cmul(*p8, *ff[j])
            nf.append((sr + cf * ar, si + cf * ai))
            sr, si = scan8(bre[rb, col], bim[rb, col], mb, (p1, p2, p4), True)
            vr, vi = cmul(p1[0], -p1[1], sr, si)
            ar, ai = cmul(p8[0], -p8[1], *mm[j])
            nm.append((db * vr + cb * ar, db * vi + cb * ai))
        return nf, nm, prod * cf

    zero = jnp.zeros((8, LANES), F32)
    start = [(zero, zero) for _ in range(CH)]
    ff, mm, prod = lax.fori_loop(0, GROUPS, step, (start, start, zero + 1.0), unroll=2)
    rows = (
        [ff[j][0][7:8] for j in range(CH)]
        + [ff[j][1][7:8] for j in range(CH)]
        + [mm[j][0][0:1] for j in range(CH)]
        + [mm[j][1][0:1] for j in range(CH)]
        + [prod[7:8]]
    )
    for k, row in enumerate(rows):
        msg[:, :, k * LANES : (k + 1) * LANES] = jnp.broadcast_to(
            row[None], (BLOCKS, 1, LANES)
        )


def local_call(idx, par, mine, other, in_weight, out_weight):
    far = pl.BlockSpec(memory_space=pltpu.HBM)
    return pl.pallas_call(
        local_kernel,
        grid_spec=pltpu.PrefetchScalarGridSpec(
            num_scalar_prefetch=1,
            grid=(1,),
            in_specs=[
                whole((16, LANES)), whole((TOK + 8, 2 * D)), whole((TOK + 8, 2 * D)), far, far,
            ],
            out_specs=whole((BLOCKS, 1, MSG)),
            scratch_shapes=[pltpu.VMEM((T, D), BF16)] * 2
            + [pltpu.VMEM((T, W), F32)] * 4
            + [pltpu.VMEM((T, LANES), F32), pltpu.VMEM((4, D, W), BF16)]
            + [pltpu.SemaphoreType.DMA((4,))],
        ),
        out_shape=jax.ShapeDtypeStruct((BLOCKS, 1, MSG), F32),
        compiler_params=params(LOCAL_VMEM),
        name="local",
    )(idx, par, mine, other, in_weight, out_weight)


def one_hot(order):
    r = lax.broadcasted_iota(jnp.int32, (D, D), 0)
    k = lax.broadcasted_iota(jnp.int32, (D, D), 1)
    z, low = (r >> 3) & 7, r & 7
    x, v = (r >> 7, (r >> 6) & 1) if order == "xy" else ((r >> 6) & 3, r >> 8)
    old = x * 128 + z * 16 + v * 8 + low
    return jnp.where(old == k, 1.0, 0.0).astype(BF16)


def tables(p1, p2, p4, i):
    one = (jnp.ones((8, LANES), F32), jnp.zeros((8, LANES), F32))
    tr, ti = one
    for bit, p in ((1, p1), (2, p2), (4, p4)):
        nr, ni = cmul(tr, ti, *p)
        on = (i & bit) != 0
        tr, ti = jnp.where(on, nr, tr), jnp.where(on, ni, ti)
    up = cmul(tr, ti, *p1)
    tr, ti = one
    for bit, p in ((1, p1), (2, p2), (4, p4)):
        nr, ni = cmul(tr, ti, *p)
        on = ((7 - i) & bit) != 0
        tr, ti = jnp.where(on, nr, tr), jnp.where(on, ni, ti)
    return up, (tr, -ti)


def spread(a, j):
    return jnp.broadcast_to(a[j : j + 1, :], (8, LANES))


def arriving(got, dec, places, blocks, columns):
    def joined(b, carry):
        ff, mm = carry
        e = BLOCKS - 1 - b

        def row(at, k):
            return jnp.broadcast_to(got[at, :, columns(k)], (8, LANES))

        dec_f = jnp.broadcast_to(dec[pl.ds(b, 1), :], (8, LANES))
        dec_m = jnp.broadcast_to(dec[pl.ds(e, 1), :], (8, LANES))
        nf, nm = [], []
        for n, (q, j) in enumerate(places):
            pr, pi = blocks[n]
            tr, ti = cmul(dec_f * pr, dec_f * pi, *ff[n])
            on = b < q
            nf.append((
                jnp.where(on, tr + row(b, (0, j)), ff[n][0]),
                jnp.where(on, ti + row(b, (1, j)), ff[n][1]),
            ))
            tr, ti = cmul(dec_m * pr, -(dec_m * pi), *mm[n])
            on = e > q
            nm.append((
                jnp.where(on, tr + row(e, (2, j)), mm[n][0]),
                jnp.where(on, ti + row(e, (3, j)), mm[n][1]),
            ))
        return nf, nm

    zero = jnp.zeros((8, LANES), F32)
    start = [(zero, zero)] * len(places)
    return lax.fori_loop(0, BLOCKS, joined, (start, start))


def states(
    idx, par, halves, got, dec, win, wout, shift, places,
    packed, drive, sig, cot, damp, fre, fim, bre, bim, sr_, ar_, weights, sems,
    between=lambda: None,
):
    c = idx[0]
    width = fre.shape[1]
    chunks = width // LANES
    copies = []
    for k in range(4):
        first = (k % 2) * N + c * W + shift * LANES
        copies.append(
            pltpu.make_async_copy(
                (win, wout)[k // 2].at[:, pl.ds(pl.multiple_of(first, width), width)],
                weights.at[k], sems.at[k],
            )
        )
        copies[k].start()
    for k, (near, far) in enumerate(halves):
        for half, at in ((near, c), (far, 1 - c)):
            rows = pl.ds(pl.multiple_of(k * T + at * TOK, TOK), TOK)
            damp[rows, :] = jnp.broadcast_to(half[TOK : TOK + 1, :LANES], (TOK, LANES)).T
            sig[rows, :] = half[:TOK, :D].astype(BF16)
            cot[rows, :] = half[:TOK, D:].astype(BF16)
    between()
    for k, (lhs, out) in enumerate(((sig, fre), (sig, fim), (cot, bre), (cot, bim))):
        copies[k].wait()
        out[...] = jnp.dot(lhs[...], weights[k], preferred_element_type=F32)
    i = rows8()
    pw, blocks, tabs, gams = [], [], [], []
    for j in range(chunks):
        take = lambda k: jnp.broadcast_to(par[pl.ds(4 * k + shift + j, 1), :], (8, LANES))
        p1 = (take(0), take(1))
        p2 = cmul(*p1, *p1)
        p4 = cmul(*p2, *p2)
        pr, pi = cmul(*p4, *p4)
        for _ in range(5):
            pr, pi = cmul(pr, pi, pr, pi)
        pw.append((p1, p2, p4))
        blocks.append((pr, pi))
        tabs.append(tables(p1, p2, p4, i))
        gams.append(take(2))

    def columns(k):
        return pl.ds(pl.multiple_of((k[0] * CH + shift + k[1]) * LANES, LANES), LANES)

    ff, mm = arriving(
        got, dec, [(q, j) for q in places for j in range(chunks)],
        blocks * len(places), columns,
    )

    def step(g, carry):
        ff, mm = carry
        nf, nm = [], []
        for k in range(len(places)):
            rf = pl.ds(pl.multiple_of(k * T + g * 8, 8), 8)
            rb = pl.ds(pl.multiple_of(k * T + (GROUPS - 1 - g) * 8, 8), 8)
            df, db = damp[rf, :], damp[rb, :]
            mf, mb = fwd_factors(df, i), bwd_factors(db, i)
            cf = cum_fwd(df, i)
            cb = cum_bwd(jnp.where(i < 7, pltpu.roll(db, 7, 0), 1.0), i)
            for j in range(chunks):
                n = chunks * k + j
                col = pl.ds(j * LANES, LANES)
                colb = pl.ds(width + j * LANES, LANES)
                p1 = pw[j][0]
                sr, si = scan8(
                    gams[j] * fre[rf, col], gams[j] * fim[rf, col], mf, pw[j], False
                )
                tr, ti = cmul(*tabs[j][0], *ff[n])
                sr, si = sr + cf * tr, si + cf * ti
                sr_[rf, col] = sr
                sr_[rf, colb] = si
                nf.append((spread(sr, 7), spread(si, 7)))
                vr, vi = scan8(bre[rb, col], bim[rb, col], mb, pw[j], True)
                tr, ti = cmul(*tabs[j][1], *mm[n])
                vr, vi = vr + cb * tr, vi + cb * ti
                ar_[rb, col] = gams[j] * vr
                ar_[rb, colb] = gams[j] * vi
                tr, ti = cmul(p1[0], -p1[1], vr, vi)
                nm.append((spread(db * tr, 0), spread(db * ti, 0)))
        return nf, nm

    lax.fori_loop(0, GROUPS, step, (ff, mm))
    packed[...] = sr_[...].astype(BF16)
    drive[...] = ar_[...].astype(BF16)


def scratch(tokens, width):
    return (
        [pltpu.VMEM((tokens, D), BF16)] * 2
        + [pltpu.VMEM((tokens, LANES), F32)]
        + [pltpu.VMEM((tokens, width), F32)] * 4
        + [pltpu.VMEM((tokens, 2 * width), F32)] * 2
        + [pltpu.VMEM((4, D, width), BF16), pltpu.SemaphoreType.DMA((4,))]
    )


def pair_kernel(
    idx, par, mine, other, pmine, pother, got, dec, win, wout,
    first, second, packed, drive, lhs_in, lhs_out, *rest,
):
    x, v, w, q = idx[1], idx[2], idx[3], idx[4]
    sig, cot = rest[:2]

    def turned():
        lhs_in[...] = lax.dot_general(
            one_hot("xy"), sig[...], NT, preferred_element_type=F32
        ).astype(BF16)
        lhs_out[...] = lax.dot_general(
            one_hot("yx"), cot[...], NT, preferred_element_type=F32
        ).astype(BF16)

    states(
        idx, par, ((mine, other), (pmine, pother)), got, dec, win, wout, 2 * w, (q, q ^ 1),
        packed, drive, *rest, between=turned,
    )
    second[...] = jnp.dot(lhs_out[side(1 - v), :], packed[...], preferred_element_type=F32)
    first[...] = jnp.dot(lhs_in[part(x, 2), :], drive[...], preferred_element_type=F32)


def part(at, d):
    return pl.ds(pl.multiple_of(((at + d) & 3) * 128, 128), 128)


def side(at):
    return pl.ds(pl.multiple_of(at * 256, 256), 256)


def pair_call(idx, par, mine, other, pmine, pother, got, dec, in_weight, out_weight):
    shapes = [((128, 2 * H), F32), ((256, 2 * H), F32)]
    shapes += [((2 * T, 2 * H), BF16)] * 2 + [((D, 2 * T), BF16)] * 2
    far = pl.BlockSpec(memory_space=pltpu.HBM)
    return pl.pallas_call(
        pair_kernel,
        grid_spec=pltpu.PrefetchScalarGridSpec(
            num_scalar_prefetch=1,
            grid=(1,),
            in_specs=[whole((16, LANES))] + [whole((TOK + 8, 2 * D))] * 4
            + [whole((BLOCKS, 1, MSG)), whole((BLOCKS, LANES)), far, far],
            out_specs=[whole(s) for s, _ in shapes],
            scratch_shapes=scratch(2 * T, H),
        ),
        out_shape=[jax.ShapeDtypeStruct(s, t) for s, t in shapes],
        compiler_params=params(PAIR_VMEM),
        name="pair",
    )(idx, par, mine, other, pmine, pother, got, dec, in_weight, out_weight)


def grads_kernel(idx, par, mine, other, got, dec, win, wout, packed, drive, *rest):
    states(
        idx, par, ((mine, other),), got, dec, win, wout, 0, (idx[4],), packed, drive, *rest
    )


def params(limit=VMEM):
    return pltpu.CompilerParams(vmem_limit_bytes=limit)


def whole(shape):
    return pl.BlockSpec(shape, lambda s, ix: (0,) * len(shape))


def grads_call(idx, par, mine, other, got, dec, in_weight, out_weight):
    far = pl.BlockSpec(memory_space=pltpu.HBM)
    return pl.pallas_call(
        grads_kernel,
        grid_spec=pltpu.PrefetchScalarGridSpec(
            num_scalar_prefetch=1,
            grid=(1,),
            in_specs=[
                whole((16, LANES)), whole((TOK + 8, 2 * D)), whole((TOK + 8, 2 * D)),
                whole((BLOCKS, 1, MSG)), whole((BLOCKS, LANES)), far, far,
            ],
            out_specs=[whole((T, 2 * W))] * 2,
            scratch_shapes=scratch(T, W),
        ),
        out_shape=[jax.ShapeDtypeStruct((T, 2 * W), BF16)] * 2,
        compiler_params=params(),
        name="grads",
    )(idx, par, mine, other, got, dec, in_weight, out_weight)


def second_kernel(idx, drive, lhs_in, first1, first3):
    for d, first in ((1, first1), (3, first3)):
        first[...] = jnp.dot(
            lhs_in[part(idx[1], d), :], drive[...], preferred_element_type=F32
        )


def second_call(idx, drive, lhs_in):
    return pl.pallas_call(
        second_kernel,
        grid_spec=pltpu.PrefetchScalarGridSpec(
            num_scalar_prefetch=1,
            grid=(1,),
            in_specs=[whole((2 * T, 2 * H)), whole((D, 2 * T))],
            out_specs=[whole((128, 2 * H))] * 2,
        ),
        out_shape=[jax.ShapeDtypeStruct((128, 2 * H), F32)] * 2,
        compiler_params=params(),
        name="second",
    )(idx, drive, lhs_in)


def chunk_kernel(idx, packed, drive, lhs_in, lhs_out, first, second):
    first[...] = jnp.dot(lhs_in[part(idx[1], 0), :], drive[...], preferred_element_type=F32)
    second[...] = jnp.dot(lhs_out[side(idx[2]), :], packed[...], preferred_element_type=F32)


def chunk_call(idx, packed, drive, lhs_in, lhs_out):
    shapes = [(128, 2 * H), (256, 2 * H)]
    return pl.pallas_call(
        chunk_kernel,
        grid_spec=pltpu.PrefetchScalarGridSpec(
            num_scalar_prefetch=1,
            grid=(1,),
            in_specs=[whole((2 * T, 2 * H))] * 2 + [whole((D, 2 * T))] * 2,
            out_specs=[whole(s) for s in shapes],
        ),
        out_shape=[jax.ShapeDtypeStruct(s, F32) for s in shapes],
        compiler_params=params(),
        name="chunk",
    )(idx, packed, drive, lhs_in, lhs_out)


def rows_kernel(idx, packed, drive, win_re, win_im, wout_re, wout_im, own, oth):
    c = idx[0]
    for out, at in ((own, c), (oth, 1 - c)):
        rows = pl.ds(pl.multiple_of(at * TOK, TOK), TOK)
        out[:, :D] = lax.dot_general(
            packed[rows, :W], wout_re[...], NT, preferred_element_type=F32
        ) + lax.dot_general(packed[rows, W:], wout_im[...], NT, preferred_element_type=F32)
        out[:, D:] = lax.dot_general(
            drive[rows, :W], win_re[...], NT, preferred_element_type=F32
        ) + lax.dot_general(drive[rows, W:], win_im[...], NT, preferred_element_type=F32)


def rows_call(idx, packed, drive, in_weight, out_weight):
    half = lambda k: pl.BlockSpec((D, W), lambda s, ix: (0, k * C + ix[0]))
    return pl.pallas_call(
        rows_kernel,
        grid_spec=pltpu.PrefetchScalarGridSpec(
            num_scalar_prefetch=1,
            grid=(1,),
            in_specs=[
                whole((T, 2 * W)), whole((T, 2 * W)), half(0), half(1), half(0), half(1),
            ],
            out_specs=[whole((TOK, 2 * D))] * 2,
        ),
        out_shape=[jax.ShapeDtypeStruct((TOK, 2 * D), F32)] * 2,
        compiler_params=params(),
        name="rows",
    )(idx, packed, drive, in_weight, in_weight, out_weight, out_weight)


def gathered(parts, at, count):
    out = []
    for k in range(count):
        first = ((at + k) & (count - 1)) * 64
        out.append(sum(lax.dynamic_slice(p, (first, 0), (64, 2 * H)) for p in parts))
    return out


def joined_kernel(a0, a1, b0, b1, b2, b3, out):
    out[:, 0:4, :] = (a0[...] + a1[...]).reshape(2 * Z, 4, 2 * H)
    total = b0[...] + b1[...] + b2[...] + b3[...]
    out[:, 4:8, :] = total.reshape(2 * Z, 4, 2 * H)


def joined_call(one, two):
    return pl.pallas_call(
        joined_kernel,
        out_shape=jax.ShapeDtypeStruct((2 * Z, 8, 2 * H), F32),
        compiler_params=params(),
        name="joined",
    )(*one, *two)


def tail_kernel(idx, keep, come, grad_in, grad_out):
    c = idx[0]
    for piece, at in ((keep, c), (come, 1 - c)):
        for k, out in enumerate((grad_in, grad_out)):
            for h in range(2):
                for w in range(2):
                    cols = pl.ds(pl.multiple_of(h * N + at * W + w * H, H), H)
                    out[:, cols] = piece[w, k, :, h * H : (h + 1) * H]


def tail_call(idx, keep, come):
    return pl.pallas_call(
        tail_kernel,
        grid_spec=pltpu.PrefetchScalarGridSpec(
            num_scalar_prefetch=1,
            grid=(1,),
            in_specs=[whole((2, 2, 2, 2 * H))] * 2,
            out_specs=[whole((2, 2 * N))] * 2,
        ),
        out_shape=[jax.ShapeDtypeStruct((2, 2 * N), F32)] * 2,
        compiler_params=params(),
        name="tail",
    )(idx, keep, come)


def body(signal, damping, nu_log, theta, in_weight, out_weight, skip_gain, cotangent):
    x, z, v = lax.axis_index("x"), lax.axis_index("z"), lax.axis_index("v")
    w, c = lax.axis_index("w"), lax.axis_index("c")
    idx = jnp.stack([c, x, v, w, z * Y + 2 * v + w]).astype(jnp.int32)
    rate = jnp.exp(nu_log)
    magnitude = jnp.exp(-rate)
    par = jnp.concatenate(
        [magnitude * jnp.cos(theta), magnitude * jnp.sin(theta), jnp.sqrt(-jnp.expm1(-2.0 * rate)), rate]
    ).reshape(4, C, CH, LANES)
    par = lax.dynamic_index_in_dim(par, c, 1, False).reshape(16, LANES)
    sig, cot = signal[0], cotangent[0]
    mine = (
        jnp.pad(sig.astype(F32), ((0, 8), (0, D)))
        + jnp.pad(cot.astype(F32), ((0, 8), (D, 0)))
        + jnp.pad(damping, ((TOK, 7), (0, 2 * D - TOK)))
    )
    swap = ring(C, 1)
    other = lax.ppermute(mine, "c", swap)
    pair = ring(2, 1)
    pmine = lax.ppermute(mine, "w", pair)
    pother = lax.ppermute(other, "w", pair)
    msg = local_call(
        idx, par, mine, other, in_weight, out_weight
    )
    got = lax.all_to_all(msg, ("z", "v", "w"), 0, 0)
    dec = jnp.maximum(got[:, 0, 4 * W :], 0.0)
    first2, far, packed2, drive2, lhs_in, lhs_out = pair_call(
        idx, par, mine, other, pmine, pother, got, dec, in_weight, out_weight
    )

    def hop(piece, axis, size, d):
        return lax.ppermute(piece, axis, ring(size, d))

    two = [hop(far, "v", 2, 1)]
    one = [hop(first2, "x", X, 2)]
    first1, first3 = second_call(idx, drive2, lhs_in)
    one += [hop(first1, "x", X, 1), hop(first3, "x", X, 3)]
    first, second = chunk_call(idx, packed2, drive2, lhs_in, lhs_out)
    two = gathered([second] + two, x, X)
    two = [two[0]] + [hop(two[d], "x", X, d) for d in (2, 1, 3)]
    one = gathered([first] + one, v, 2)
    one = [one[0], hop(one[1], "v", 2, 1)]
    packed, drive = grads_call(idx, par, mine, other, got, dec, in_weight, out_weight)
    own, oth = rows_call(idx, packed, drive, in_weight, out_weight)
    own = own + lax.ppermute(oth, "c", swap)
    gain = jnp.concatenate([skip_gain, skip_gain])
    rows = (own + gain * mine[:TOK]).astype(BF16)
    small = joined_call(one, two)
    small = lax.all_to_all(small, ("z", "w"), 0, 0)
    small = small.reshape(Z, 2, 2, C, 2, 2 * H).sum(0)
    keep = lax.dynamic_index_in_dim(small, c, 2, False)
    send = lax.dynamic_index_in_dim(small, 1 - c, 2, False)
    come = lax.ppermute(send, "c", swap)
    grad_in, grad_out = tail_call(idx, keep, come)
    return rows[None, :, :D], rows[None, :, D:], grad_in, grad_out


def solution(mesh):
    grid = Mesh(np.asarray(mesh.devices).reshape(X, Z, 2, 2, C), ("x", "z", "v", "w", "c"))
    tm = ("z", "v", "w", "c")
    placed = (P("x", tm, None), P("x", tm), P(), P(), P(), P(), P(), P("x", tm, None))
    rows = P(("x",) + tm, None)

    return jax.shard_map(
        body,
        mesh=grid,
        in_specs=placed,
        out_specs=(P("x", tm, None), P("x", tm, None), rows, rows),
        check_vma=False,
    )
```

```python
import jax
import jax.numpy as jnp
import numpy as np
from jax import lax
from jax.experimental import pallas as pl
from jax.experimental.pallas import tpu as pltpu
from jax.sharding import Mesh, PartitionSpec as P


X, Z, Y, C = 4, 8, 4, 2
D, N = 512, 1024
TOK = 128
T = C * TOK
W = N // C
H = W // 2
LANES = 128
CH = W // LANES
GROUPS = T // 8
BLOCKS = Z * Y
F32, BF16 = jnp.float32, jnp.bfloat16
NT = (((1,), (1,)), ((), ()))
VMEM = 24 << 20
PAIR_VMEM = 24 << 20
LOCAL_VMEM = 51 << 20
MSG = 4 * W + LANES


def ring(size, step):
    return [(i, (i + step) % size) for i in range(size)]


def cmul(ar, ai, br, bi):
    return ar * br - ai * bi, ar * bi + ai * br


def rows8():
    return lax.broadcasted_iota(jnp.int32, (8, LANES), 0)


def fwd_factors(d, i):
    dd = d * pltpu.roll(d, 1, 0)
    dddd = dd * pltpu.roll(dd, 2, 0)
    m1 = jnp.where(i >= 1, d, 0.0)
    m2 = jnp.where(i >= 2, dd, 0.0)
    m4 = jnp.where(i >= 4, dddd, 0.0)
    return m1, m2, m4


def cum_fwd(d, i):
    p = d
    for k in (1, 2, 4):
        p = jnp.where(i >= k, p * pltpu.roll(p, k, 0), p)
    return p


def cum_bwd(d, i):
    p = d
    for k in (1, 2, 4):
        p = jnp.where(i < 8 - k, p * pltpu.roll(p, 8 - k, 0), p)
    return p


def bwd_factors(d, i):
    e = pltpu.roll(d, 7, 0)
    ee = e * pltpu.roll(e, 7, 0)
    eeee = ee * pltpu.roll(ee, 6, 0)
    m1 = jnp.where(i < 7, e, 0.0)
    m2 = jnp.where(i < 6, ee, 0.0)
    m4 = jnp.where(i < 4, eeee, 0.0)
    return m1, m2, m4


def scan8(sr, si, masks, powers, backward):
    for (k, m), (pr, pi) in zip(zip((1, 2, 4), masks), powers):
        shift = 8 - k if backward else k
        rr = m * pltpu.roll(sr, shift, 0)
        ri = m * pltpu.roll(si, shift, 0)
        if backward:
            sr, si = sr + (pr * rr + pi * ri), si + (pr * ri - pi * rr)
        else:
            sr, si = sr + (pr * rr - pi * ri), si + (pr * ri + pi * rr)
    return sr, si


def powers_of(par_ref, j):
    lr = jnp.broadcast_to(par_ref[j : j + 1, :], (8, LANES))
    li = jnp.broadcast_to(par_ref[4 + j : 5 + j, :], (8, LANES))
    p1 = (lr, li)
    p2 = cmul(*p1, *p1)
    p4 = cmul(*p2, *p2)
    p8 = cmul(*p4, *p4)
    return p1, p2, p4, p8


def local_kernel(
    idx, par, mine, other, win, wout, msg,
    sig_all, cot_all, fre, fim, bre, bim, damp, weights, sems,
):
    c = idx[0]
    copies = []
    for k in range(4):
        cols = pl.ds(pl.multiple_of((k % 2) * N + c * W, W), W)
        copies.append(
            pltpu.make_async_copy(
                (win, wout)[k // 2].at[:, cols], weights.at[k], sems.at[k]
            )
        )
        copies[k].start()
    own = pl.ds(pl.multiple_of(c * TOK, TOK), TOK)
    oth = pl.ds(pl.multiple_of((1 - c) * TOK, TOK), TOK)
    for at, half in ((own, mine), (oth, other)):
        damp[at, :] = jnp.broadcast_to(half[TOK : TOK + 1, :LANES], (TOK, LANES)).T
        sig_all[at, :] = half[:TOK, :D].astype(BF16)
        cot_all[at, :] = half[:TOK, D:].astype(BF16)
    s = sig_all[...]
    u = cot_all[...]
    for k, (lhs, out) in enumerate(((s, fre), (s, fim), (u, bre), (u, bim))):
        copies[k].wait()
        out[...] = jnp.dot(lhs, weights[k], preferred_element_type=F32)
    i = rows8()
    pw = [powers_of(par, j) for j in range(CH)]
    gam = [jnp.broadcast_to(par[8 + j : 9 + j, :], (8, LANES)) for j in range(CH)]

    def step(g, carry):
        ff, mm, prod = carry
        rf = pl.ds(pl.multiple_of(g * 8, 8), 8)
        rb = pl.ds(pl.multiple_of((GROUPS - 1 - g) * 8, 8), 8)
        df = damp[rf, :]
        db = damp[rb, :]
        mf = fwd_factors(df, i)
        mb = bwd_factors(db, i)
        cf = cum_fwd(df, i)
        cb = cum_bwd(db, i)
        nf, nm = [], []
        for j in range(CH):
            col = pl.ds(j * LANES, LANES)
            p1, p2, p4, p8 = pw[j]
            sr, si = scan8(
                gam[j] * fre[rf, col], gam[j] * fim[rf, col], mf, (p1, p2, p4), False
            )
            ar, ai = cmul(*p8, *ff[j])
            nf.append((sr + cf * ar, si + cf * ai))
            sr, si = scan8(bre[rb, col], bim[rb, col], mb, (p1, p2, p4), True)
            vr, vi = cmul(p1[0], -p1[1], sr, si)
            ar, ai = cmul(p8[0], -p8[1], *mm[j])
            nm.append((db * vr + cb * ar, db * vi + cb * ai))
        return nf, nm, prod * cf

    zero = jnp.zeros((8, LANES), F32)
    start = [(zero, zero) for _ in range(CH)]
    ff, mm, prod = lax.fori_loop(0, GROUPS, step, (start, start, zero + 1.0), unroll=2)
    rows = (
        [ff[j][0][7:8] for j in range(CH)]
        + [ff[j][1][7:8] for j in range(CH)]
        + [mm[j][0][0:1] for j in range(CH)]
        + [mm[j][1][0:1] for j in range(CH)]
        + [prod[7:8]]
    )
    for k, row in enumerate(rows):
        msg[:, :, k * LANES : (k + 1) * LANES] = jnp.broadcast_to(
            row[None], (BLOCKS, 1, LANES)
        )


def local_call(idx, par, mine, other, in_weight, out_weight):
    far = pl.BlockSpec(memory_space=pltpu.HBM)
    return pl.pallas_call(
        local_kernel,
        grid_spec=pltpu.PrefetchScalarGridSpec(
            num_scalar_prefetch=1,
            grid=(1,),
            in_specs=[
                whole((16, LANES)), whole((TOK + 8, 2 * D)), whole((TOK + 8, 2 * D)), far, far,
            ],
            out_specs=whole((BLOCKS, 1, MSG)),
            scratch_shapes=[pltpu.VMEM((T, D), BF16)] * 2
            + [pltpu.VMEM((T, W), F32)] * 4
            + [pltpu.VMEM((T, LANES), F32), pltpu.VMEM((4, D, W), BF16)]
            + [pltpu.SemaphoreType.DMA((4,))],
        ),
        out_shape=jax.ShapeDtypeStruct((BLOCKS, 1, MSG), F32),
        compiler_params=params(LOCAL_VMEM),
        name="local",
    )(idx, par, mine, other, in_weight, out_weight)


def one_hot(order):
    r = lax.broadcasted_iota(jnp.int32, (D, D), 0)
    k = lax.broadcasted_iota(jnp.int32, (D, D), 1)
    z, low = (r >> 3) & 7, r & 7
    x, v = (r >> 7, (r >> 6) & 1) if order == "xy" else ((r >> 6) & 3, r >> 8)
    old = x * 128 + z * 16 + v * 8 + low
    return jnp.where(old == k, 1.0, 0.0).astype(BF16)


def tables(p1, p2, p4, i):
    one = (jnp.ones((8, LANES), F32), jnp.zeros((8, LANES), F32))
    tr, ti = one
    for bit, p in ((1, p1), (2, p2), (4, p4)):
        nr, ni = cmul(tr, ti, *p)
        on = (i & bit) != 0
        tr, ti = jnp.where(on, nr, tr), jnp.where(on, ni, ti)
    up = cmul(tr, ti, *p1)
    tr, ti = one
    for bit, p in ((1, p1), (2, p2), (4, p4)):
        nr, ni = cmul(tr, ti, *p)
        on = ((7 - i) & bit) != 0
        tr, ti = jnp.where(on, nr, tr), jnp.where(on, ni, ti)
    return up, (tr, -ti)


def spread(a, j):
    return jnp.broadcast_to(a[j : j + 1, :], (8, LANES))


def arriving(got, dec, places, blocks, columns):
    def joined(b, carry):
        ff, mm = carry
        e = BLOCKS - 1 - b

        def row(at, k):
            return jnp.broadcast_to(got[at, :, columns(k)], (8, LANES))

        dec_f = jnp.broadcast_to(dec[pl.ds(b, 1), :], (8, LANES))
        dec_m = jnp.broadcast_to(dec[pl.ds(e, 1), :], (8, LANES))
        nf, nm = [], []
        for n, (q, j) in enumerate(places):
            pr, pi = blocks[n]
            tr, ti = cmul(dec_f * pr, dec_f * pi, *ff[n])
            on = b < q
            nf.append((
                jnp.where(on, tr + row(b, (0, j)), ff[n][0]),
                jnp.where(on, ti + row(b, (1, j)), ff[n][1]),
            ))
            tr, ti = cmul(dec_m * pr, -(dec_m * pi), *mm[n])
            on = e > q
            nm.append((
                jnp.where(on, tr + row(e, (2, j)), mm[n][0]),
                jnp.where(on, ti + row(e, (3, j)), mm[n][1]),
            ))
        return nf, nm

    zero = jnp.zeros((8, LANES), F32)
    start = [(zero, zero)] * len(places)
    return lax.fori_loop(0, BLOCKS, joined, (start, start))


def states(
    idx, par, halves, got, dec, win, wout, shift, places,
    packed, drive, sig, cot, damp, fre, fim, bre, bim, sr_, ar_, weights, sems,
    between=lambda: None,
):
    c = idx[0]
    width = fre.shape[1]
    chunks = width // LANES
    copies = []
    for k in range(4):
        first = (k % 2) * N + c * W + shift * LANES
        copies.append(
            pltpu.make_async_copy(
                (win, wout)[k // 2].at[:, pl.ds(pl.multiple_of(first, width), width)],
                weights.at[k], sems.at[k],
            )
        )
        copies[k].start()
    for k, (near, far) in enumerate(halves):
        for half, at in ((near, c), (far, 1 - c)):
            rows = pl.ds(pl.multiple_of(k * T + at * TOK, TOK), TOK)
            damp[rows, :] = jnp.broadcast_to(half[TOK : TOK + 1, :LANES], (TOK, LANES)).T
            sig[rows, :] = half[:TOK, :D].astype(BF16)
            cot[rows, :] = half[:TOK, D:].astype(BF16)
    between()
    for k, (lhs, out) in enumerate(((sig, fre), (sig, fim), (cot, bre), (cot, bim))):
        copies[k].wait()
        out[...] = jnp.dot(lhs[...], weights[k], preferred_element_type=F32)
    i = rows8()
    pw, blocks, tabs, gams = [], [], [], []
    for j in range(chunks):
        take = lambda k: jnp.broadcast_to(par[pl.ds(4 * k + shift + j, 1), :], (8, LANES))
        p1 = (take(0), take(1))
        p2 = cmul(*p1, *p1)
        p4 = cmul(*p2, *p2)
        pr, pi = cmul(*p4, *p4)
        for _ in range(5):
            pr, pi = cmul(pr, pi, pr, pi)
        pw.append((p1, p2, p4))
        blocks.append((pr, pi))
        tabs.append(tables(p1, p2, p4, i))
        gams.append(take(2))

    def columns(k):
        return pl.ds(pl.multiple_of((k[0] * CH + shift + k[1]) * LANES, LANES), LANES)

    ff, mm = arriving(
        got, dec, [(q, j) for q in places for j in range(chunks)],
        blocks * len(places), columns,
    )

    def step(g, carry):
        ff, mm = carry
        nf, nm = [], []
        for k in range(len(places)):
            rf = pl.ds(pl.multiple_of(k * T + g * 8, 8), 8)
            rb = pl.ds(pl.multiple_of(k * T + (GROUPS - 1 - g) * 8, 8), 8)
            df, db = damp[rf, :], damp[rb, :]
            mf, mb = fwd_factors(df, i), bwd_factors(db, i)
            cf = cum_fwd(df, i)
            cb = cum_bwd(jnp.where(i < 7, pltpu.roll(db, 7, 0), 1.0), i)
            for j in range(chunks):
                n = chunks * k + j
                col = pl.ds(j * LANES, LANES)
                colb = pl.ds(width + j * LANES, LANES)
                p1 = pw[j][0]
                sr, si = scan8(
                    gams[j] * fre[rf, col], gams[j] * fim[rf, col], mf, pw[j], False
                )
                tr, ti = cmul(*tabs[j][0], *ff[n])
                sr, si = sr + cf * tr, si + cf * ti
                sr_[rf, col] = sr
                sr_[rf, colb] = si
                nf.append((spread(sr, 7), spread(si, 7)))
                vr, vi = scan8(bre[rb, col], bim[rb, col], mb, pw[j], True)
                tr, ti = cmul(*tabs[j][1], *mm[n])
                vr, vi = vr + cb * tr, vi + cb * ti
                ar_[rb, col] = gams[j] * vr
                ar_[rb, colb] = gams[j] * vi
                tr, ti = cmul(p1[0], -p1[1], vr, vi)
                nm.append((spread(db * tr, 0), spread(db * ti, 0)))
        return nf, nm

    lax.fori_loop(0, GROUPS, step, (ff, mm))
    packed[...] = sr_[...].astype(BF16)
    drive[...] = ar_[...].astype(BF16)


def scratch(tokens, width):
    return (
        [pltpu.VMEM((tokens, D), BF16)] * 2
        + [pltpu.VMEM((tokens, LANES), F32)]
        + [pltpu.VMEM((tokens, width), F32)] * 4
        + [pltpu.VMEM((tokens, 2 * width), F32)] * 2
        + [pltpu.VMEM((4, D, width), BF16), pltpu.SemaphoreType.DMA((4,))]
    )


def pair_kernel(
    idx, par, mine, other, pmine, pother, got, dec, win, wout,
    first, second, packed, drive, lhs_in, lhs_out, *rest,
):
    x, v, w, q = idx[1], idx[2], idx[3], idx[4]
    sig, cot = rest[:2]

    def turned():
        lhs_in[...] = lax.dot_general(
            one_hot("xy"), sig[...], NT, preferred_element_type=F32
        ).astype(BF16)
        lhs_out[...] = lax.dot_general(
            one_hot("yx"), cot[...], NT, preferred_element_type=F32
        ).astype(BF16)

    states(
        idx, par, ((mine, other), (pmine, pother)), got, dec, win, wout, 2 * w, (q, q ^ 1),
        packed, drive, *rest, between=turned,
    )
    second[...] = jnp.dot(lhs_out[side(1 - v), :], packed[...], preferred_element_type=F32)
    first[...] = jnp.dot(lhs_in[part(x, 2), :], drive[...], preferred_element_type=F32)


def part(at, d):
    return pl.ds(pl.multiple_of(((at + d) & 3) * 128, 128), 128)


def side(at):
    return pl.ds(pl.multiple_of(at * 256, 256), 256)


def pair_call(idx, par, mine, other, pmine, pother, got, dec, in_weight, out_weight):
    shapes = [((128, 2 * H), F32), ((256, 2 * H), F32)]
    shapes += [((2 * T, 2 * H), BF16)] * 2 + [((D, 2 * T), BF16)] * 2
    far = pl.BlockSpec(memory_space=pltpu.HBM)
    return pl.pallas_call(
        pair_kernel,
        grid_spec=pltpu.PrefetchScalarGridSpec(
            num_scalar_prefetch=1,
            grid=(1,),
            in_specs=[whole((16, LANES))] + [whole((TOK + 8, 2 * D))] * 4
            + [whole((BLOCKS, 1, MSG)), whole((BLOCKS, LANES)), far, far],
            out_specs=[whole(s) for s, _ in shapes],
            scratch_shapes=scratch(2 * T, H),
        ),
        out_shape=[jax.ShapeDtypeStruct(s, t) for s, t in shapes],
        compiler_params=params(PAIR_VMEM),
        name="pair",
    )(idx, par, mine, other, pmine, pother, got, dec, in_weight, out_weight)


def grads_kernel(idx, par, mine, other, got, dec, win, wout, own, oth, packed, drive, *rest):
    states(
        idx, par, ((mine, other),), got, dec, win, wout, 0, (idx[4],), packed, drive, *rest
    )
    weights = rest[-2]
    for out, at in ((own, idx[0]), (oth, 1 - idx[0])):
        rows = pl.ds(pl.multiple_of(at * TOK, TOK), TOK)
        for k, (lhs, cols) in enumerate(((packed, pl.ds(0, D)), (drive, pl.ds(D, D)))):
            re, im = (weights[2], weights[3]) if k == 0 else (weights[0], weights[1])
            out[:, cols] = lax.dot_general(
                lhs[rows, :W], re, NT, preferred_element_type=F32
            ) + lax.dot_general(lhs[rows, W:], im, NT, preferred_element_type=F32)


def params(limit=VMEM):
    return pltpu.CompilerParams(vmem_limit_bytes=limit)


def whole(shape):
    return pl.BlockSpec(shape, lambda s, ix: (0,) * len(shape))


def grads_call(idx, par, mine, other, got, dec, in_weight, out_weight):
    far = pl.BlockSpec(memory_space=pltpu.HBM)
    return pl.pallas_call(
        grads_kernel,
        grid_spec=pltpu.PrefetchScalarGridSpec(
            num_scalar_prefetch=1,
            grid=(1,),
            in_specs=[
                whole((16, LANES)), whole((TOK + 8, 2 * D)), whole((TOK + 8, 2 * D)),
                whole((BLOCKS, 1, MSG)), whole((BLOCKS, LANES)), far, far,
            ],
            out_specs=[whole((TOK, 2 * D))] * 2,
            scratch_shapes=[pltpu.VMEM((T, 2 * W), BF16)] * 2 + scratch(T, W),
        ),
        out_shape=[jax.ShapeDtypeStruct((TOK, 2 * D), F32)] * 2,
        compiler_params=params(),
        name="grads",
    )(idx, par, mine, other, got, dec, in_weight, out_weight)


def second_kernel(
    idx, packed, drive, lhs_in, lhs_out, first1, first3, first, second,
):
    for d, out in ((1, first1), (3, first3), (0, first)):
        out[...] = jnp.dot(
            lhs_in[part(idx[1], d), :], drive[...], preferred_element_type=F32
        )
    second[...] = jnp.dot(lhs_out[side(idx[2]), :], packed[...], preferred_element_type=F32)


def second_call(idx, packed, drive, lhs_in, lhs_out):
    shapes = [(128, 2 * H)] * 3 + [(256, 2 * H)]
    return pl.pallas_call(
        second_kernel,
        grid_spec=pltpu.PrefetchScalarGridSpec(
            num_scalar_prefetch=1,
            grid=(1,),
            in_specs=[whole((2 * T, 2 * H))] * 2 + [whole((D, 2 * T))] * 2,
            out_specs=[whole(s) for s in shapes],
        ),
        out_shape=[jax.ShapeDtypeStruct(s, F32) for s in shapes],
        compiler_params=params(),
        name="second",
    )(idx, packed, drive, lhs_in, lhs_out)


def gathered(parts, at, count):
    out = []
    for k in range(count):
        first = ((at + k) & (count - 1)) * 64
        out.append(sum(lax.dynamic_slice(p, (first, 0), (64, 2 * H)) for p in parts))
    return out


def joined_kernel(a0, a1, b0, b1, b2, b3, out):
    out[:, 0:4, :] = (a0[...] + a1[...]).reshape(2 * Z, 4, 2 * H)
    total = b0[...] + b1[...] + b2[...] + b3[...]
    out[:, 4:8, :] = total.reshape(2 * Z, 4, 2 * H)


def joined_call(one, two):
    return pl.pallas_call(
        joined_kernel,
        out_shape=jax.ShapeDtypeStruct((2 * Z, 8, 2 * H), F32),
        compiler_params=params(),
        name="joined",
    )(*one, *two)


def tail_kernel(idx, keep, come, grad_in, grad_out):
    c = idx[0]
    for piece, at in ((keep, c), (come, 1 - c)):
        for k, out in enumerate((grad_in, grad_out)):
            for h in range(2):
                for w in range(2):
                    cols = pl.ds(pl.multiple_of(h * N + at * W + w * H, H), H)
                    out[:, cols] = piece[w, k, :, h * H : (h + 1) * H]


def tail_call(idx, keep, come):
    return pl.pallas_call(
        tail_kernel,
        grid_spec=pltpu.PrefetchScalarGridSpec(
            num_scalar_prefetch=1,
            grid=(1,),
            in_specs=[whole((2, 2, 2, 2 * H))] * 2,
            out_specs=[whole((2, 2 * N))] * 2,
        ),
        out_shape=[jax.ShapeDtypeStruct((2, 2 * N), F32)] * 2,
        compiler_params=params(),
        name="tail",
    )(idx, keep, come)


def body(signal, damping, nu_log, theta, in_weight, out_weight, skip_gain, cotangent):
    x, z, v = lax.axis_index("x"), lax.axis_index("z"), lax.axis_index("v")
    w, c = lax.axis_index("w"), lax.axis_index("c")
    idx = jnp.stack([c, x, v, w, z * Y + 2 * v + w]).astype(jnp.int32)
    rate = jnp.exp(nu_log)
    magnitude = jnp.exp(-rate)
    par = jnp.concatenate(
        [magnitude * jnp.cos(theta), magnitude * jnp.sin(theta), jnp.sqrt(-jnp.expm1(-2.0 * rate)), rate]
    ).reshape(4, C, CH, LANES)
    par = lax.dynamic_index_in_dim(par, c, 1, False).reshape(16, LANES)
    sig, cot = signal[0], cotangent[0]
    mine = (
        jnp.pad(sig.astype(F32), ((0, 8), (0, D)))
        + jnp.pad(cot.astype(F32), ((0, 8), (D, 0)))
        + jnp.pad(damping, ((TOK, 7), (0, 2 * D - TOK)))
    )
    swap = ring(C, 1)
    other = lax.ppermute(mine, "c", swap)
    pair = ring(2, 1)
    pmine = lax.ppermute(mine, "w", pair)
    pother = lax.ppermute(other, "w", pair)
    msg = local_call(
        idx, par, mine, other, in_weight, out_weight
    )
    got = lax.all_to_all(msg, ("z", "v", "w"), 0, 0)
    dec = jnp.maximum(got[:, 0, 4 * W :], 0.0)
    first2, far, packed2, drive2, lhs_in, lhs_out = pair_call(
        idx, par, mine, other, pmine, pother, got, dec, in_weight, out_weight
    )

    def hop(piece, axis, size, d):
        return lax.ppermute(piece, axis, ring(size, d))

    two = [hop(far, "v", 2, 1)]
    one = [hop(first2, "x", X, 2)]
    first1, first3, first, second = second_call(idx, packed2, drive2, lhs_in, lhs_out)
    one += [hop(first1, "x", X, 1), hop(first3, "x", X, 3)]
    two = gathered([second] + two, x, X)
    two = [two[0]] + [hop(two[d], "x", X, d) for d in (2, 1, 3)]
    one = gathered([first] + one, v, 2)
    one = [one[0], hop(one[1], "v", 2, 1)]
    own, oth = grads_call(idx, par, mine, other, got, dec, in_weight, out_weight)
    own = own + lax.ppermute(oth, "c", swap)
    gain = jnp.concatenate([skip_gain, skip_gain])
    rows = (own + gain * mine[:TOK]).astype(BF16)
    small = joined_call(one, two)
    small = lax.all_to_all(small, ("z", "w"), 0, 0)
    small = small.reshape(Z, 2, 2, C, 2, 2 * H).sum(0)
    keep = lax.dynamic_index_in_dim(small, c, 2, False)
    send = lax.dynamic_index_in_dim(small, 1 - c, 2, False)
    come = lax.ppermute(send, "c", swap)
    grad_in, grad_out = tail_call(idx, keep, come)
    return rows[None, :, :D], rows[None, :, D:], grad_in, grad_out


def solution(mesh):
    grid = Mesh(np.asarray(mesh.devices).reshape(X, Z, 2, 2, C), ("x", "z", "v", "w", "c"))
    tm = ("z", "v", "w", "c")
    placed = (P("x", tm, None), P("x", tm), P(), P(), P(), P(), P(), P("x", tm, None))
    rows = P(("x",) + tm, None)

    return jax.shard_map(
        body,
        mesh=grid,
        in_specs=placed,
        out_specs=(P("x", tm, None), P("x", tm, None), rows, rows),
        check_vma=False,
    )
```

```python
import jax
import jax.numpy as jnp
import numpy as np
from jax import lax
from jax.experimental import pallas as pl
from jax.experimental.pallas import tpu as pltpu
from jax.sharding import Mesh, PartitionSpec as P


X, Z, Y, C = 4, 8, 4, 2
D, N = 512, 1024
TOK = 128
T = C * TOK
W = N // C
LANES = 128
CH = W // LANES
GROUPS = T // 8
BLOCKS = Z * Y
F32, BF16 = jnp.float32, jnp.bfloat16
NT = (((1,), (1,)), ((), ()))
VMEM = 20 << 20
LOCAL_VMEM = 49 << 20
MSG = 4 * W + LANES


def ring(size, step):
    return [(i, (i + step) % size) for i in range(size)]


def cmul(ar, ai, br, bi):
    return ar * br - ai * bi, ar * bi + ai * br


def rows8():
    return lax.broadcasted_iota(jnp.int32, (8, LANES), 0)


def fwd_factors(d, i):
    dd = d * pltpu.roll(d, 1, 0)
    dddd = dd * pltpu.roll(dd, 2, 0)
    m1 = jnp.where(i >= 1, d, 0.0)
    m2 = jnp.where(i >= 2, dd, 0.0)
    m4 = jnp.where(i >= 4, dddd, 0.0)
    return m1, m2, m4


def cum_fwd(d, i):
    p = d
    for k in (1, 2, 4):
        p = jnp.where(i >= k, p * pltpu.roll(p, k, 0), p)
    return p


def cum_bwd(d, i):
    p = d
    for k in (1, 2, 4):
        p = jnp.where(i < 8 - k, p * pltpu.roll(p, 8 - k, 0), p)
    return p


def bwd_factors(d, i):
    e = pltpu.roll(d, 7, 0)
    ee = e * pltpu.roll(e, 7, 0)
    eeee = ee * pltpu.roll(ee, 6, 0)
    m1 = jnp.where(i < 7, e, 0.0)
    m2 = jnp.where(i < 6, ee, 0.0)
    m4 = jnp.where(i < 4, eeee, 0.0)
    return m1, m2, m4


def scan8(sr, si, masks, powers, backward):
    for (k, m), (pr, pi) in zip(zip((1, 2, 4), masks), powers):
        shift = 8 - k if backward else k
        rr = m * pltpu.roll(sr, shift, 0)
        ri = m * pltpu.roll(si, shift, 0)
        if backward:
            sr, si = sr + (pr * rr + pi * ri), si + (pr * ri - pi * rr)
        else:
            sr, si = sr + (pr * rr - pi * ri), si + (pr * ri + pi * rr)
    return sr, si


def powers_of(par_ref, j):
    lr = jnp.broadcast_to(par_ref[j : j + 1, :], (8, LANES))
    li = jnp.broadcast_to(par_ref[4 + j : 5 + j, :], (8, LANES))
    p1 = (lr, li)
    p2 = cmul(*p1, *p1)
    p4 = cmul(*p2, *p2)
    p8 = cmul(*p4, *p4)
    return p1, p2, p4, p8


def local_kernel(
    idx, par, mine, other, win, wout,
    sig_all, cot_all, fre, fim, bre, bim, msg, damp, weights, sems,
):
    c = idx[0]
    copies = []
    for k in range(4):
        cols = pl.ds(pl.multiple_of((k % 2) * N + c * W, W), W)
        copies.append(
            pltpu.make_async_copy(
                (win, wout)[k // 2].at[:, cols], weights.at[k], sems.at[k]
            )
        )
        copies[k].start()
    own = pl.ds(pl.multiple_of(c * TOK, TOK), TOK)
    oth = pl.ds(pl.multiple_of((1 - c) * TOK, TOK), TOK)
    for at, half in ((own, mine), (oth, other)):
        damp[at, :] = jnp.broadcast_to(half[TOK : TOK + 1, :LANES], (TOK, LANES)).T
        sig_all[at, :] = half[:TOK, :D].astype(BF16)
        cot_all[at, :] = half[:TOK, D:].astype(BF16)
    s = sig_all[...]
    u = cot_all[...]
    for k, (lhs, out) in enumerate(((s, fre), (s, fim), (u, bre), (u, bim))):
        copies[k].wait()
        out[...] = jnp.dot(lhs, weights[k], preferred_element_type=F32)
    i = rows8()
    pw = [powers_of(par, j) for j in range(CH)]
    gam = [jnp.broadcast_to(par[8 + j : 9 + j, :], (8, LANES)) for j in range(CH)]

    def step(g, carry):
        ff, mm, prod = carry
        rf = pl.ds(pl.multiple_of(g * 8, 8), 8)
        rb = pl.ds(pl.multiple_of((GROUPS - 1 - g) * 8, 8), 8)
        df = damp[rf, :]
        db = damp[rb, :]
        mf = fwd_factors(df, i)
        mb = bwd_factors(db, i)
        cf = cum_fwd(df, i)
        cb = cum_bwd(db, i)
        nf, nm = [], []
        for j in range(CH):
            col = pl.ds(j * LANES, LANES)
            p1, p2, p4, p8 = pw[j]
            sr, si = scan8(
                gam[j] * fre[rf, col], gam[j] * fim[rf, col], mf, (p1, p2, p4), False
            )
            fre[rf, col] = sr
            fim[rf, col] = si
            ar, ai = cmul(*p8, *ff[j])
            nf.append((sr + cf * ar, si + cf * ai))
            sr, si = scan8(bre[rb, col], bim[rb, col], mb, (p1, p2, p4), True)
            bre[rb, col] = sr
            bim[rb, col] = si
            vr, vi = cmul(p1[0], -p1[1], sr, si)
            ar, ai = cmul(p8[0], -p8[1], *mm[j])
            nm.append((db * vr + cb * ar, db * vi + cb * ai))
        return nf, nm, prod * cf

    zero = jnp.zeros((8, LANES), F32)
    start = [(zero, zero) for _ in range(CH)]
    ff, mm, prod = lax.fori_loop(0, GROUPS, step, (start, start, zero + 1.0), unroll=2)
    rows = (
        [ff[j][0][7:8] for j in range(CH)]
        + [ff[j][1][7:8] for j in range(CH)]
        + [mm[j][0][0:1] for j in range(CH)]
        + [mm[j][1][0:1] for j in range(CH)]
        + [prod[7:8]]
    )
    for k, row in enumerate(rows):
        msg[:, :, k * LANES : (k + 1) * LANES] = jnp.broadcast_to(
            row[None], (BLOCKS, 1, LANES)
        )


def local_call(idx, par, mine, other, in_weight, out_weight):
    shapes = (
        [((T, D), BF16)] * 2 + [((T, W), F32)] * 4
        + [((BLOCKS, 1, MSG), F32), ((T, LANES), F32)]
    )
    far = pl.BlockSpec(memory_space=pltpu.HBM)
    return pl.pallas_call(
        local_kernel,
        grid_spec=pltpu.PrefetchScalarGridSpec(
            num_scalar_prefetch=1,
            grid=(1,),
            in_specs=[
                whole((16, LANES)), whole((TOK + 8, 2 * D)), whole((TOK + 8, 2 * D)), far, far,
            ],
            out_specs=[whole(s) for s, _ in shapes],
            scratch_shapes=[pltpu.VMEM((4, D, W), BF16), pltpu.SemaphoreType.DMA((4,))],
        ),
        out_shape=[jax.ShapeDtypeStruct(s, t) for s, t in shapes],
        compiler_params=params(LOCAL_VMEM),
        name="local",
    )(idx, par, mine, other, in_weight, out_weight)


def one_hot(order):
    r = lax.broadcasted_iota(jnp.int32, (D, D), 0)
    k = lax.broadcasted_iota(jnp.int32, (D, D), 1)
    hi, mid, z, low = r >> 7, (r >> 5) & 3, (r >> 2) & 7, r & 3
    x, y = (hi, mid) if order == "xy" else (mid, hi)
    old = x * 128 + z * 16 + y * 4 + low
    return jnp.where(old == k, 1.0, 0.0).astype(BF16)


def grads_kernel(
    idx, par, damp, sig, cot, fre, fim, bre, bim, got,
    first, second, packed, drive, lhs_in, lhs_out, sr_, ar_,
):
    x, y, q = idx[1], idx[2], idx[3]
    i = rows8()
    blocks = []
    for j in range(CH):
        pr, pi = powers_of(par, j)[3]
        for _ in range(5):
            pr, pi = cmul(pr, pi, pr, pi)
        blocks.append((pr, pi))

    def row(b, k):
        return jnp.broadcast_to(got[b, :, k * LANES : (k + 1) * LANES], (8, LANES))

    def joined(b, carry):
        ff, mm = carry
        e = BLOCKS - 1 - b
        dec_f, dec_m = row(b, 4 * CH), row(e, 4 * CH)
        nf, nm = [], []
        for j in range(CH):
            pr, pi = blocks[j]
            tr, ti = cmul(dec_f * pr, dec_f * pi, *ff[j])
            on = b < q
            nf.append((
                jnp.where(on, tr + row(b, j), ff[j][0]),
                jnp.where(on, ti + row(b, CH + j), ff[j][1]),
            ))
            tr, ti = cmul(dec_m * pr, -(dec_m * pi), *mm[j])
            on = e > q
            nm.append((
                jnp.where(on, tr + row(e, 2 * CH + j), mm[j][0]),
                jnp.where(on, ti + row(e, 3 * CH + j), mm[j][1]),
            ))
        return nf, nm

    zero = jnp.zeros((8, LANES), F32)
    ff, mm = lax.fori_loop(0, BLOCKS, joined, ([(zero, zero)] * CH, [(zero, zero)] * CH))
    spread = lambda a, j: jnp.broadcast_to(a[j : j + 1, :], (8, LANES))
    tabs, backs, gams, ones = [], [], [], []
    for j in range(CH):
        p1, p2, p4, _ = powers_of(par, j)
        tr, ti = zero8 = (jnp.ones((8, LANES), F32), jnp.zeros((8, LANES), F32))
        for bit, p in ((1, p1), (2, p2), (4, p4)):
            nr, ni = cmul(tr, ti, *p)
            on = (i & bit) != 0
            tr, ti = jnp.where(on, nr, tr), jnp.where(on, ni, ti)
        tabs.append(cmul(tr, ti, *p1))
        tr, ti = zero8
        for bit, p in ((1, p1), (2, p2), (4, p4)):
            nr, ni = cmul(tr, ti, *p)
            on = ((7 - i) & bit) != 0
            tr, ti = jnp.where(on, nr, tr), jnp.where(on, ni, ti)
        backs.append((tr, -ti))
        gams.append(jnp.broadcast_to(par[8 + j : 9 + j, :], (8, LANES)))
        ones.append(p1)

    def step(g, carry):
        ff, mm = carry
        rf = pl.ds(pl.multiple_of(g * 8, 8), 8)
        rb = pl.ds(pl.multiple_of((GROUPS - 1 - g) * 8, 8), 8)
        cf = cum_fwd(damp[rf, :], i)
        db = damp[rb, :]
        e = jnp.where(i < 7, pltpu.roll(db, 7, 0), 1.0)
        cb = cum_bwd(e, i)
        nf, nm = [], []
        for j in range(CH):
            col = pl.ds(j * LANES, LANES)
            colb = pl.ds(W + j * LANES, LANES)
            tr, ti = cmul(*tabs[j], *ff[j])
            sr = fre[rf, col] + cf * tr
            si = fim[rf, col] + cf * ti
            sr_[rf, col] = sr
            sr_[rf, colb] = si
            nf.append((spread(sr, 7), spread(si, 7)))
            tr, ti = cmul(*backs[j], *mm[j])
            vr = bre[rb, col] + cb * tr
            vi = bim[rb, col] + cb * ti
            ar_[rb, col] = gams[j] * vr
            ar_[rb, colb] = gams[j] * vi
            tr, ti = cmul(ones[j][0], -ones[j][1], vr, vi)
            nm.append((spread(db * tr, 0), spread(db * ti, 0)))
        return nf, nm

    lax.fori_loop(0, GROUPS, step, (ff, mm), unroll=2)
    packed[...] = sr_[...].astype(BF16)
    drive[...] = ar_[...].astype(BF16)
    lhs_in[...] = lax.dot_general(
        one_hot("xy"), sig[...], NT, preferred_element_type=F32
    ).astype(BF16)
    lhs_out[...] = lax.dot_general(
        one_hot("yx"), cot[...], NT, preferred_element_type=F32
    ).astype(BF16)
    first[...] = jnp.dot(lhs_in[part(x, 2), :], drive[...], preferred_element_type=F32)
    second[...] = jnp.dot(lhs_out[part(y, 2), :], packed[...], preferred_element_type=F32)


def part(at, d):
    return pl.ds(pl.multiple_of(((at + d) & 3) * 128, 128), 128)


def params(limit=VMEM):
    return pltpu.CompilerParams(vmem_limit_bytes=limit)


def whole(shape):
    return pl.BlockSpec(shape, lambda s, ix: (0,) * len(shape))


def grads_call(idx, par, damp, sig, cot, fre, fim, bre, bim, got):
    shapes = [((128, 2 * W), F32)] * 2 + [((T, 2 * W), BF16)] * 2 + [((D, T), BF16)] * 2
    return pl.pallas_call(
        grads_kernel,
        grid_spec=pltpu.PrefetchScalarGridSpec(
            num_scalar_prefetch=1,
            grid=(1,),
            in_specs=[
                whole((16, LANES)), whole((T, LANES)), whole((T, D)), whole((T, D)),
                whole((T, W)), whole((T, W)), whole((T, W)), whole((T, W)),
                whole((BLOCKS, 1, MSG)),
            ],
            out_specs=[whole(s) for s, _ in shapes],
            scratch_shapes=[pltpu.VMEM((T, 2 * W), F32), pltpu.VMEM((T, 2 * W), F32)],
        ),
        out_shape=[jax.ShapeDtypeStruct(s, t) for s, t in shapes],
        compiler_params=params(),
        name="grads",
    )(idx, par, damp, sig, cot, fre, fim, bre, bim, got)


def second_kernel(idx, packed, drive, lhs_in, lhs_out, first1, second1, first3, second3):
    x, y = idx[1], idx[2]
    for d, first, second in ((1, first1, second1), (3, first3, second3)):
        first[...] = jnp.dot(lhs_in[part(x, d), :], drive[...], preferred_element_type=F32)
        second[...] = jnp.dot(lhs_out[part(y, d), :], packed[...], preferred_element_type=F32)


def second_call(idx, packed, drive, lhs_in, lhs_out):
    return pl.pallas_call(
        second_kernel,
        grid_spec=pltpu.PrefetchScalarGridSpec(
            num_scalar_prefetch=1,
            grid=(1,),
            in_specs=[whole((T, 2 * W)), whole((T, 2 * W)), whole((D, T)), whole((D, T))],
            out_specs=[whole((128, 2 * W))] * 4,
        ),
        out_shape=[jax.ShapeDtypeStruct((128, 2 * W), F32)] * 4,
        compiler_params=params(),
        name="second",
    )(idx, packed, drive, lhs_in, lhs_out)


def rows_kernel(
    idx, packed, drive, lhs_in, lhs_out, win_re, win_im, wout_re, wout_im,
    own, oth, first, second,
):
    c, x, y = idx[0], idx[1], idx[2]
    first[...] = jnp.dot(lhs_in[part(x, 0), :], drive[...], preferred_element_type=F32)
    second[...] = jnp.dot(lhs_out[part(y, 0), :], packed[...], preferred_element_type=F32)
    for out, at in ((own, c), (oth, 1 - c)):
        rows = pl.ds(pl.multiple_of(at * TOK, TOK), TOK)
        out[:, :D] = lax.dot_general(
            packed[rows, :W], wout_re[...], NT, preferred_element_type=F32
        ) + lax.dot_general(packed[rows, W:], wout_im[...], NT, preferred_element_type=F32)
        out[:, D:] = lax.dot_general(
            drive[rows, :W], win_re[...], NT, preferred_element_type=F32
        ) + lax.dot_general(drive[rows, W:], win_im[...], NT, preferred_element_type=F32)


def rows_call(idx, packed, drive, lhs_in, lhs_out, in_weight, out_weight):
    half = lambda k: pl.BlockSpec((D, W), lambda s, ix: (0, k * C + ix[0]))
    return pl.pallas_call(
        rows_kernel,
        grid_spec=pltpu.PrefetchScalarGridSpec(
            num_scalar_prefetch=1,
            grid=(1,),
            in_specs=[
                whole((T, 2 * W)), whole((T, 2 * W)), whole((D, T)), whole((D, T)),
                half(0), half(1), half(0), half(1),
            ],
            out_specs=[whole((TOK, 2 * D))] * 4,
        ),
        out_shape=[jax.ShapeDtypeStruct((TOK, 2 * D), F32)] * 4,
        compiler_params=params(),
        name="rows",
    )(idx, packed, drive, lhs_in, lhs_out, in_weight, in_weight, out_weight, out_weight)


def gathered(parts, at):
    out = []
    for k in range(4):
        first = ((at + k) & 3) * 32
        out.append(sum(lax.dynamic_slice(p, (first, 0), (32, 2 * W)) for p in parts))
    return out


def joined_kernel(a0, a1, a2, a3, b0, b1, b2, b3, out):
    for k, parts in enumerate(((a0, a1, a2, a3), (b0, b1, b2, b3))):
        total = parts[0][...] + parts[1][...] + parts[2][...] + parts[3][...]
        out[:, 4 * k : 4 * k + 4, :] = total.reshape(Z, 4, 2 * W)


def joined_call(one, two):
    return pl.pallas_call(
        joined_kernel,
        out_shape=jax.ShapeDtypeStruct((Z, 8, 2 * W), F32),
        compiler_params=params(),
        name="joined",
    )(*one, *two)


def tail_kernel(idx, keep, come, grad_in, grad_out):
    c = idx[0]
    for part, at in ((keep, c), (come, 1 - c)):
        for k, out in enumerate((grad_in, grad_out)):
            for h in range(2):
                cols = pl.ds(pl.multiple_of(h * N + at * W, W), W)
                out[:, cols] = part[k, :, h * W : (h + 1) * W]


def tail_call(idx, keep, come):
    return pl.pallas_call(
        tail_kernel,
        grid_spec=pltpu.PrefetchScalarGridSpec(
            num_scalar_prefetch=1,
            grid=(1,),
            in_specs=[whole((2, 2, 2 * W))] * 2,
            out_specs=[whole((2, 2 * N))] * 2,
        ),
        out_shape=[jax.ShapeDtypeStruct((2, 2 * N), F32)] * 2,
        compiler_params=params(),
        name="tail",
    )(idx, keep, come)


def body(signal, damping, nu_log, theta, in_weight, out_weight, skip_gain, cotangent):
    x, z = lax.axis_index("x"), lax.axis_index("z")
    y, c = lax.axis_index("y"), lax.axis_index("c")
    idx = jnp.stack([c, x, y, z * Y + y]).astype(jnp.int32)
    rate = jnp.exp(nu_log)
    magnitude = jnp.exp(-rate)
    par = jnp.concatenate(
        [magnitude * jnp.cos(theta), magnitude * jnp.sin(theta), jnp.sqrt(-jnp.expm1(-2.0 * rate)), rate]
    ).reshape(4, C, CH, LANES)
    par = lax.dynamic_index_in_dim(par, c, 1, False).reshape(16, LANES)
    sig, cot = signal[0], cotangent[0]
    mine = (
        jnp.pad(sig.astype(F32), ((0, 8), (0, D)))
        + jnp.pad(cot.astype(F32), ((0, 8), (D, 0)))
        + jnp.pad(damping, ((TOK, 7), (0, 2 * D - TOK)))
    )
    swap = ring(C, 1)
    other = lax.ppermute(mine, "c", swap)
    sig_all, cot_all, fre, fim, bre, bim, msg, damp = local_call(
        idx, par, mine, other, in_weight, out_weight
    )
    got = lax.all_to_all(msg, ("z", "y"), 0, 0)
    first2, second2, packed, drive, lhs_in, lhs_out = grads_call(
        idx, par, damp, sig_all, cot_all, fre, fim, bre, bim, got
    )

    def hop(part, axis, d):
        return lax.ppermute(part, axis, ring(4, d))

    one, two = [hop(first2, "x", 2)], [hop(second2, "y", 2)]
    first1, second1, first3, second3 = second_call(idx, packed, drive, lhs_in, lhs_out)
    one += [hop(first1, "x", 1), hop(first3, "x", 3)]
    two += [hop(second1, "y", 1), hop(second3, "y", 3)]
    own, oth, first, second = rows_call(
        idx, packed, drive, lhs_in, lhs_out, in_weight, out_weight
    )
    own = own + lax.ppermute(oth, "c", swap)
    gain = jnp.concatenate([skip_gain, skip_gain])
    rows = (own + gain * mine[:TOK]).astype(BF16)
    one = gathered([first] + one, y)
    one = [one[0]] + [hop(one[d], "y", d) for d in (2, 1, 3)]
    two = gathered([second] + two, x)
    two = [two[0]] + [hop(two[d], "x", d) for d in (2, 1, 3)]
    small = joined_call(one, two)
    small = lax.all_to_all(small, "z", 0, 0).sum(0).reshape(2, C, 2, 2 * W)
    keep = lax.dynamic_index_in_dim(small, c, 1, False)
    send = lax.dynamic_index_in_dim(small, 1 - c, 1, False)
    come = lax.ppermute(send, "c", swap)
    grad_in, grad_out = tail_call(idx, keep, come)
    return rows[None, :, :D], rows[None, :, D:], grad_in, grad_out


def solution(mesh):
    grid = Mesh(np.asarray(mesh.devices).reshape(X, Z, Y, C), ("x", "z", "y", "c"))
    tm = ("z", "y", "c")
    placed = (P("x", tm, None), P("x", tm), P(), P(), P(), P(), P(), P("x", tm, None))
    rows = P(("x",) + tm, None)

    return jax.shard_map(
        body,
        mesh=grid,
        in_specs=placed,
        out_specs=(P("x", tm, None), P("x", tm, None), rows, rows),
        check_vma=False,
    )
```
